32 devices in a mesh: grp: 4 (over y, x), dev: 8 (over z, core).
Axes of the slice: x: 2, y: 2, z: 4, core: 2. Of those that a mesh axis runs over, the one named last changes fastest.
Arguments:
- face_owner: int32 [131072, 1], P(('grp', 'dev')), may hold values from 0 to 31; in each aligned block of 4096 rows (0 to 4095, 4096 to 8191, ...) at most 256 rows name the same one
- face_element: int32 [131072], P(('grp', 'dev')), may hold values from 0 to 16383
- element_state: bfloat16 [110, 131072], P(None, ('grp', 'dev')), may hold values from -6 to 6
- lift: bfloat16 [30, 110], replicated, may hold values from -0.5 to 0.5
- face_scale: float32 [131072], P(('grp', 'dev')), may hold values from 0.5 to 2
- transfer: float32 [4, 10], replicated, may hold values from 0.05 to 0.5
- stiffness_ref: float32 [12, 12], replicated, may hold values from -0.18 to 5, as said below
- element_scale: float32 [256, 2048], P('grp', 'dev'), may hold values from 1 to 1.1
- displacement_prev: float32 [4, 3, 256, 2048], P(None, None, 'grp', 'dev'), may hold values from -6 to 6
Outputs:
- shell_displacement: float32 [4, 3, 256, 2048], P(None, None, 'grp', 'dev')
- face_displacement: float32 [3, 10, 131072], P(None, None, ('grp', 'dev'))
The draws below stay inside these ranges and needn't reach their ends.
Inputs may be any that keep to these rules, and one draw needn't show every extreme that they name: `face_owner`: among the 4096 faces of one device (aligned blocks), at most 256 name the same owner, and in every draw some device has exactly 256 faces on one owner. `stiffness_ref`: every diagonal entry is 5 and the off-diagonal entries of each row have absolute values summing to at most 2.
All inputs are finite; a program needn't handle non-finite values.
Results may differ from the reference program's by a relative error of at most 0.0003.
Values sent between devices are 32-bit elements; how exact they have to be, the bound alone decides.
A program may use at most 128 MiB of HBM per device.

```python
import math
import jax
import jax.numpy as jnp
import numpy as np
from jax import lax

NODES_F = 10
STATE = 110
SWEEPS = 8
FACES_DEV = 4096
SX = 64
SY = 256
CAP = 256
FACES = 131072
N_GRP = 4
N_DEV = 8
DEVICES = 32


def draw_stiffness_ref(key, part):
    key_one = jax.random.fold_in(jax.random.fold_in(key, 7), 0)
    spread = jax.random.uniform(key_one, (12, 12), jnp.float32, -0.18, 0.18)
    identity = jnp.eye(12, dtype=jnp.float32)
    return spread * (1.0 - identity) + 5.0 * identity


def set_ends(result, rng, low, high):
    shape = result.shape
    place = [jax.random.randint(jax.random.fold_in(rng, axis), (), 0, shape[axis]) for axis in range(len(shape))]
    result = result.at[tuple(place)].set(low)
    longest = shape.index(max(shape))
    place[longest] = (place[longest] + 1) % shape[longest]
    return result.at[tuple(place)].set(high)


def block_scale(rng, dims, shards, low, top_value):
    def one(position, blocks):
        draws = jax.random.uniform(jax.random.fold_in(jax.random.fold_in(rng, 6), position), (blocks,), jnp.float32, low / len(shards), top_value / len(shards))
        return jnp.repeat(jnp.exp(draws), dims[position] // blocks).reshape((-1,) + (1,) * (len(dims) - position - 1))

    factor_of = one(*shards[0])
    for cut in shards[1:]:
        factor_of = factor_of * one(*cut)
    return factor_of


def assign_block(rng, own, number, rows, number_of, top, reach, skew):
    sequence = jax.random.permutation(rng, number_of)
    packed, ordinary = shares(number_of, rows * top, reach, skew, True), shares(number_of, rows * top, reach, skew, False)
    places = jnp.arange(number_of)

    def named(sizes, turn):
        used = int((sizes > 0).sum())
        fixed = max(1, used // 4)
        moved = fixed + (places - fixed + turn * (used - fixed)) % max(1, number_of - fixed)
        return jnp.zeros((number_of,), jnp.int32).at[sequence[jnp.where(places < fixed, places, moved)]].set(jnp.asarray(sizes, jnp.int32))

    sizes = jnp.where(number % 4 == 0, named(packed, number // 4), named(ordinary, number - number // 4 - 1))
    mixed = jax.random.permutation(jax.random.fold_in(own, 3), number_of)
    giver, receiver = mixed[0:number_of // 2 * 2:2], mixed[1:number_of // 2 * 2:2]
    slack = jnp.minimum(sizes[giver] - 1, reach - sizes[receiver]) // 2
    slack = jnp.where((giver == sequence[0]) | (receiver == sequence[0]) | (sizes[receiver] == 0), 0, jnp.maximum(slack, 0))
    moved = jax.random.randint(jax.random.fold_in(own, 4), (number_of // 2,), 0, 1 << 20) % (slack + 1)
    sizes = sizes.at[giver].add(-moved).at[receiver].add(moved)
    labels = jnp.searchsorted(jnp.cumsum(sizes), jnp.arange(rows * top), side="right").astype(jnp.int32)
    listing = labels.reshape(top, rows).T
    listing = listing[jax.random.permutation(jax.random.fold_in(own, 1), rows)]
    turn = jax.random.randint(jax.random.fold_in(own, 2), (rows, 1), 0, top)
    return jnp.take_along_axis(listing, (jnp.arange(top)[None, :] + turn) % top, axis=1)


def shares(number_of, total, limit, skew, full):
    weights = [(1 << 20) // math.isqrt(rank ** skew) + 1 for rank in range(1, number_of + 1)]
    largest = limit if full else min(limit, max(-(-total // number_of), total * weights[0] // sum(weights)))
    least = 1 if total - largest >= number_of - 1 else 0
    given, spare = [largest] + [least] * (number_of - 1), total - largest - least * (number_of - 1)
    while spare > 0:
        free = [i for i in range(1, number_of) if given[i] < largest] or [i for i in range(1, number_of) if given[i] < limit]
        mass, budget = sum([weights[i] for i in free]), spare
        for i in free:
            extra = min(limit - given[i], max(1, budget * weights[i] // mass), spare)
            given[i] = given[i] + extra
            spare = spare - extra
    return np.array(given)


def normal_values(rng, shape, width, most, cuts=(), kind=jnp.bfloat16):
    entries = width * jax.random.normal(rng, shape, jnp.float32)
    if cuts:
        entries = entries * block_scale(rng, shape, cuts, -0.22, 0.18)
    return jnp.clip(entries, -most, most).astype(kind)


def setup_inputs(seed: int = 0) -> dict:
    key_of = jax.random.split(jax.random.key(seed), 10)
    face_owner_keys = jax.random.split(jax.random.fold_in(key_of[0], 1), FACES // FACES_DEV)
    face_owner_turns = jax.random.permutation(jax.random.fold_in(key_of[0], 3), FACES // FACES_DEV)
    face_owner = jax.vmap(lambda own, number: assign_block(jax.random.fold_in(key_of[0], 2), own, number, FACES_DEV, DEVICES, 1, CAP, 1))(face_owner_keys, face_owner_turns).reshape((FACES, 1))
    face_element = set_ends(jax.random.randint(key_of[1], (FACES,), 0, SX * SY), jax.random.fold_in(key_of[1], 1), 0, (SX * SY) - 1).astype(jnp.int32)
    element_state = normal_values(key_of[2], (STATE, FACES), 1.0, 6.0, ((1, 32),))
    lift = normal_values(key_of[3], (3 * NODES_F, STATE), STATE ** -0.5, 0.5)
    face_scale = jnp.clip(jnp.exp(math.log(2.0) - 1.3862944 * jax.random.uniform(key_of[4], (FACES,), jnp.float32) ** block_scale(key_of[4], (FACES,), ((0, 32),), -0.2, 0.2)), 0.5, 2.0)
    transfer = jnp.clip(jax.random.uniform(key_of[5], (4, NODES_F), jnp.float32, 0.05, 0.5), 0.05, 0.5)
    stiffness_ref = draw_stiffness_ref(jax.random.fold_in(key_of[9], 71), 0)
    element_scale = jnp.clip(jnp.exp(math.log(1.1) - 0.095310201 * jax.random.uniform(key_of[7], (SX * N_GRP, SY * N_DEV), jnp.float32) ** block_scale(key_of[7], (SX * N_GRP, SY * N_DEV), ((0, 4), (1, 8)), -0.2, 0.2)), 1.0, 1.1)
    displacement_prev = normal_values(key_of[8], (4, 3, SX * N_GRP, SY * N_DEV), 1.0, 6.0, ((2, 4), (3, 8)), jnp.float32)
    return dict(face_owner=face_owner, face_element=face_element, element_state=element_state, lift=lift, face_scale=face_scale, transfer=transfer, stiffness_ref=stiffness_ref, element_scale=element_scale, displacement_prev=displacement_prev)


coupling_weight = 2.2
highest = lax.Precision.HIGHEST


def invert_block(stiffness_ref):
    identity = jnp.eye(12, dtype=jnp.float32)
    approx = identity / 5.0
    for turn_index in range(8):
        product = jnp.dot(stiffness_ref, approx, precision=highest, preferred_element_type=jnp.float32)
        approx = jnp.dot(approx, 2.0 * identity - product, precision=highest, preferred_element_type=jnp.float32)
    return approx


def couple(padded):
    east_side = padded[:, :, 1:-1, 2:]
    west_side = padded[:, :, 1:-1, :-2]
    north_side = padded[:, :, 2:, 1:-1]
    south_side = padded[:, :, :-2, 1:-1]
    return jnp.stack([west_side[1] + south_side[2], east_side[0] + south_side[3],
                      west_side[3] + north_side[0], east_side[2] + north_side[1]])


def jacobi_sweep(displacement, padded, shell_load, block_inverse, element_scale):
    right_side = shell_load + coupling_weight * couple(padded)
    solved = jnp.dot(block_inverse, right_side.reshape(12, -1), precision=highest, preferred_element_type=jnp.float32)
    return solved.reshape(displacement.shape) / element_scale


def reference(face_owner, face_element, element_state, lift, face_scale, transfer, stiffness_ref, element_scale, displacement_prev):
    traces = jnp.dot(lift, element_state, preferred_element_type=jnp.float32) * face_scale[None, :]
    traction = traces.reshape(3, NODES_F, -1)
    face_load = jnp.einsum("nk,ckf->ncf", transfer, traction, precision=highest).reshape(12, -1)
    owners = face_owner[:, 0]
    grid_width = SY * N_DEV
    grid_row = (owners // N_DEV) * SX + face_element // SY
    grid_col = (owners % N_DEV) * SY + face_element % SY
    target = (grid_row * grid_width + grid_col).astype(jnp.int32)
    shell_load = jnp.zeros((12, SX * N_GRP * grid_width), jnp.float32).at[:, target].add(face_load)
    shell_load = shell_load.reshape(4, 3, SX * N_GRP, grid_width)
    block_inverse = invert_block(stiffness_ref)
    displacement = displacement_prev
    for turn_index in range(SWEEPS):
        padded = jnp.pad(displacement, ((0, 0), (0, 0), (1, 1), (1, 1)))
        displacement = jacobi_sweep(displacement, padded, shell_load, block_inverse, element_scale)
    node_disp = displacement.reshape(12, -1)[:, target].reshape(4, 3, -1)
    face_displacement = jnp.einsum("nk,ncf->ckf", transfer, node_disp, precision=highest)
    return displacement, face_displacement
```

```python
import functools

import jax
import jax.numpy as jnp
from jax import lax
from jax.experimental import pallas as pl
from jax.experimental.pallas import tpu as pltpu
from jax.sharding import PartitionSpec as P

NODES_F = 10
SWEEPS = 8
LANES = 128
VMEM_LIMIT = 56 * 1024 * 1024

coupling_weight = 2.2
highest = lax.Precision.HIGHEST
F32 = jnp.float32
BF16 = jnp.bfloat16
NT = (((1,), (1,)), ((), ()))
VM = pl.BlockSpec(memory_space=pltpu.VMEM)
SM = pl.BlockSpec(memory_space=pltpu.SMEM)


def split(x):
    high = x.astype(BF16).astype(F32)
    return high, x - high


def one_hot(row, count):
    places = lax.broadcasted_iota(jnp.int32, (count, row.shape[1]), 0).astype(F32)
    return jnp.where(places == row, 1.0, 0.0).astype(BF16)


MESH = pl.DeviceIdType.MESH
ANY = pl.BlockSpec(memory_space=pl.ANY)
BLOCK = 8
CHUNK = 512


def triple(x):
    high = x.astype(BF16)
    rest = x - high.astype(F32)
    middle = rest.astype(BF16)
    return high, middle, (rest - middle.astype(F32)).astype(BF16)


def exact(a, b, dims=(((1,), (0,)), ((), ()))):
    return lax.dot_general(a, b, dims, precision=highest, preferred_element_type=F32)


def same(shape, of_row, of_col):
    left = of_row(lax.broadcasted_iota(jnp.int32, shape, 0))
    return left == of_col(lax.broadcasted_iota(jnp.int32, shape, 1))


def pick(shape, of_row, of_col):
    return jnp.where(same(shape, of_row, of_col), 1.0, 0.0).astype(F32)


def place_of(cap):
    halves = cap // LANES
    return halves, -(-12 * halves // 8) * 8


def identity_of(t, members):
    return (t // members, lax.rem(t, members))


def greet_all(n, members, me):
    barrier = pltpu.get_barrier_semaphore()

    def greet(k, carry):
        pl.semaphore_signal(
            barrier, inc=1, device_id=identity_of(lax.rem(me + k, n), members), device_id_type=MESH
        )
        return carry

    lax.fori_loop(1, n, greet, 0)
    return barrier


def outward_kernel(n, members, cap, rows, cols, owner_ref, element_ref, state_ref, lift_ref, scale_ref,
                   transfer_ref, stiff_ref, prev_ref, factor_ref, load_ref, edge_ref, strip_ref,
                   number_ref, rank_ref, inverse_ref, highs, lows, hots, outgoing, incoming,
                   number_out, number_in, send, recv, number_send, number_recv):
    g, d = lax.axis_index("grp"), lax.axis_index("dev")
    me = g * members + d
    barrier = greet_all(n, members, me)
    faces = owner_ref.shape[1]
    halves, deep = place_of(cap)

    spread = exact(exact(pick((16, 4), lambda i: i // 3, lambda j: j), transfer_ref[...]),
                   pick((NODES_F, 3 * NODES_F), lambda i: i, lambda j: j % NODES_F))
    kept = same(spread.shape, lambda i: i % 3, lambda j: j // NODES_F)
    kept = kept & (lax.broadcasted_iota(jnp.int32, spread.shape, 0) < 12)
    spread = jnp.where(kept, spread, 0.0)
    gather = jnp.concatenate(triple(exact(spread, lift_ref[...].astype(F32))), axis=0)
    before = jnp.where(
        lax.broadcasted_iota(jnp.int32, (CHUNK, CHUNK), 0)
        < lax.broadcasted_iota(jnp.int32, (CHUNK, CHUNK), 1), 1.0, 0.0
    ).astype(BF16)

    def rank_chunk(i, counts):
        here = pl.ds(pl.multiple_of(i * CHUNK, CHUNK), CHUNK)
        owner_hot = one_hot(owner_ref[:, here].astype(F32), n)
        running = jnp.dot(owner_hot, before, preferred_element_type=F32) + counts
        hot = owner_hot.astype(F32)
        rank = jnp.sum(hot * running, axis=0, keepdims=True)
        rank_ref[:, here] = rank
        hots[:, here] = one_hot(rank, cap)
        parts = jnp.dot(gather, state_ref[:, here], preferred_element_type=F32)
        loads = (parts[:16] + parts[16:32] + parts[32:]) * scale_ref[:, here]
        element = element_ref[:, here]
        high_row = (element // cols).astype(F32)
        low_row = (element % cols).astype(F32)
        where_row = lax.broadcasted_iota(jnp.int32, loads.shape, 0)
        values = jnp.where(where_row == 12, high_row, jnp.where(where_row == 13, low_row, loads))
        high, low = split(values)
        highs[:, here] = high
        lows[:, here] = low
        return counts + jnp.sum(hot, axis=1, keepdims=True)

    lax.fori_loop(0, faces // CHUNK, rank_chunk, jnp.zeros((n, 1), F32))
    pl.semaphore_wait(barrier, n - 1)

    def value_copy(owner, slot):
        return pltpu.make_async_remote_copy(
            src_ref=outgoing.at[owner], dst_ref=incoming.at[slot], send_sem=send.at[owner],
            recv_sem=recv.at[slot], device_id=identity_of(owner, members), device_id_type=MESH)

    def number_copy(owner, slot):
        return pltpu.make_async_remote_copy(
            src_ref=number_out.at[owner], dst_ref=number_in.at[slot], send_sem=number_send.at[owner],
            recv_sem=number_recv.at[slot], device_id=identity_of(owner, members), device_id_type=MESH)

    blocks = n // BLOCK
    mine = me // BLOCK

    def send_block(t, carry):
        first = lax.rem(mine + t, blocks) * BLOCK
        owner_wide = jnp.broadcast_to(owner_ref[...], (16, faces))
        high, low = highs[...], lows[...]
        pieces = []
        for i in range(BLOCK):
            here = owner_wide == first + i
            pieces.append(jnp.where(here, high, 0.0).astype(BF16))
            pieces.append(jnp.where(here, low, 0.0).astype(BF16))
        total = lax.dot_general(
            jnp.concatenate(pieces, axis=0), hots[...], NT, preferred_element_type=F32
        )
        for i in range(BLOCK):
            owner = first + i
            block = total[32 * i : 32 * i + 16] + total[32 * i + 16 : 32 * i + 32]
            number = (block[12:13] * cols + block[13:14]).astype(jnp.int32)
            lines = [block[:12, h * LANES : (h + 1) * LANES] for h in range(halves)]
            if deep > 12 * halves:
                lines.append(jnp.zeros((deep - 12 * halves, LANES), F32))
            block = jnp.concatenate(lines, axis=0)

            @pl.when(owner == me)
            def _():
                incoming[me] = block
                number_in[me] = number

            @pl.when(owner != me)
            def _():
                outgoing[owner] = block
                number_out[owner] = number
                number_copy(owner, me).start()
                value_copy(owner, me).start()
        return carry

    lax.fori_loop(0, blocks, send_block, 0)
    load_ref[...] = jnp.zeros_like(load_ref)

    stiffness = stiff_ref[...]
    identity = pick((12, 12), lambda i: i, lambda j: j)
    approx = identity / 5.0
    for _ in range(8):
        product = exact(stiffness, approx)
        approx = exact(approx, 2.0 * identity - product)
    inverse_ref[...] = approx

    per = max(1, min(BLOCK, 1024 // cap))
    width = per * cap

    def add_sources(t, carry):
        first = lax.rem(mine + blocks - t * per // BLOCK, blocks) * BLOCK + lax.rem(t * per, BLOCK)
        for i in range(per):

            @pl.when(first + i != me)
            def _():
                number_copy(first + i, first + i).wait_recv()
                value_copy(first + i, first + i).wait_recv()

        numbers, values = [], []
        for i in range(per):
            number = number_in[first + i]
            number_ref[first + i] = number
            numbers.append(number)
            value = incoming[first + i]
            for h in range(halves):
                values.append(value[12 * h : 12 * h + 12])
        number = jnp.concatenate(numbers, axis=1)
        value = jnp.concatenate(values, axis=1)
        mask = lax.broadcasted_iota(jnp.int32, (rows, width), 0) == number // cols
        low_hot = one_hot((number % cols).astype(F32), cols)
        high, low = split(value)
        pieces = [[], []]
        for part, kept in zip((high, low), pieces):
            for c in range(12):
                kept.append(jnp.where(mask, part[c : c + 1], 0.0).astype(BF16))
        left = jnp.concatenate(
            [jnp.concatenate(pieces[0], axis=0), jnp.concatenate(pieces[1], axis=0)], axis=1
        )
        right = jnp.concatenate([low_hot, low_hot], axis=1)
        total = lax.dot_general(left, right, NT, preferred_element_type=F32)
        load_ref[...] += total.reshape(12, rows, cols)
        return carry

    lax.fori_loop(0, n // per, add_sources, 0)

    factor = factor_ref[...]
    for side, start in ((0, 0), (1, rows - SWEEPS)):
        edge_ref[side, :12] = prev_ref[:, start : start + SWEEPS, :]
        edge_ref[side, 12] = factor[start : start + SWEEPS]
        edge_ref[side, 13:] = load_ref[:, start : start + SWEEPS, :]
    lane = lax.broadcasted_iota(jnp.int32, (rows, LANES), 1) // SWEEPS
    for side in range(2):
        base = 0 if side == 0 else cols - LANES
        turn = 0 if side == 0 else SWEEPS
        for kind in range(2):
            pieces = [(prev_ref if kind == 0 else load_ref)[c, :, base : base + LANES] for c in range(12)]
            if kind == 0:
                pieces.append(factor[:, base : base + LANES])
            packed = jnp.zeros((rows, LANES), F32)
            for j, piece in enumerate(pieces):
                move = (j * SWEEPS + turn) % LANES
                piece = pltpu.roll(piece, move, 1) if move else piece
                packed = jnp.where(lane == j, piece, packed)
            strip_ref[side, kind] = packed

    def finish(k, carry):
        owner = lax.rem(me + k, n)
        number_copy(owner, me).wait_send()
        value_copy(owner, me).wait_send()
        return carry

    lax.fori_loop(1, n, finish, 0)


def outward(cap, owner, element, state, lift, scale, transfer, stiffness, prev, factor):
    members = lax.axis_size("dev")
    n = lax.axis_size("grp") * members
    faces = owner.shape[1]
    _, rows, cols = prev.shape
    halves, deep = place_of(cap)
    shapes = [(12, rows, cols), (2, 25, SWEEPS, cols), (2, 2, rows, LANES)]
    return pl.pallas_call(
        functools.partial(outward_kernel, n, members, cap, rows, cols),
        in_specs=[VM] * 9,
        out_specs=[VM] * 6,
        out_shape=[jax.ShapeDtypeStruct(s, F32) for s in shapes]
        + [jax.ShapeDtypeStruct((n, 1, cap), jnp.int32), jax.ShapeDtypeStruct((1, faces), F32),
           jax.ShapeDtypeStruct((12, 12), F32)],
        scratch_shapes=[
            pltpu.VMEM((16, faces), F32), pltpu.VMEM((16, faces), F32), pltpu.VMEM((cap, faces), BF16),
            pltpu.VMEM((n, deep, LANES), F32), pltpu.VMEM((n, deep, LANES), F32),
            pltpu.VMEM((n, 1, cap), jnp.int32), pltpu.VMEM((n, 1, cap), jnp.int32),
        ] + [pltpu.SemaphoreType.DMA((n,))] * 4,
        compiler_params=pltpu.CompilerParams(
            collective_id=1, has_side_effects=True, vmem_limit_bytes=VMEM_LIMIT),
        name="outward",
    )(owner, element, state, lift, scale, transfer, stiffness, prev, factor)


def homeward_kernel(n, members, cap, rows, cols, disp_ref, number_ref, owner_ref, rank_ref,
                    transfer_ref, out_ref, table, hots, found, outgoing, incoming, send, recv):
    me = lax.axis_index("grp") * members + lax.axis_index("dev")
    barrier = greet_all(n, members, me)
    faces = owner_ref.shape[1]
    halves, deep = place_of(cap)
    high, low = split(disp_ref[...].reshape(12 * rows, cols))
    table[...] = jnp.concatenate([high.astype(BF16), low.astype(BF16)], axis=1)
    spread = exact(
        pick((8 * NODES_F, NODES_F), lambda i: i // 8, lambda j: j),
        exact(transfer_ref[...], pick((4, 12), lambda i: i, lambda j: j // 3), (((0,), (0,)), ((), ()))),
    )
    spread = jnp.where(same(spread.shape, lambda i: i % 8, lambda j: j % 3), spread, 0.0)
    pl.semaphore_wait(barrier, n - 1)

    def value_copy(owner, slot):
        return pltpu.make_async_remote_copy(
            src_ref=outgoing.at[owner], dst_ref=incoming.at[slot], send_sem=send.at[owner],
            recv_sem=recv.at[slot], device_id=identity_of(owner, members), device_id_type=MESH)

    blocks = n // BLOCK
    mine = me // BLOCK
    per = max(1, min(BLOCK, 1024 // cap))
    width = per * cap

    def answer(t, carry):
        first = lax.rem(mine + t * per // BLOCK, blocks) * BLOCK + lax.rem(t * per, BLOCK)
        number = jnp.concatenate([number_ref[first + i] for i in range(per)], axis=1)
        mask = lax.broadcasted_iota(jnp.int32, (rows, width), 0) == number // cols
        low_hot = one_hot((number % cols).astype(F32), cols)
        picked = jnp.dot(
            table[...], jnp.concatenate([low_hot, low_hot], axis=0), preferred_element_type=F32
        )
        lines = [
            jnp.sum(jnp.where(mask, picked[c * rows : (c + 1) * rows], 0.0), axis=0, keepdims=True)
            for c in range(12)
        ]
        result = jnp.concatenate(lines, axis=0)
        for i in range(per):
            source = first + i
            parts = [
                result[:, i * cap + h * LANES : i * cap + (h + 1) * LANES] for h in range(halves)
            ]
            if deep > 12 * halves:
                parts.append(jnp.zeros((deep - 12 * halves, LANES), F32))
            block = jnp.concatenate(parts, axis=0)

            @pl.when(source == me)
            def _():
                incoming[me] = block

            @pl.when(source != me)
            def _():
                outgoing[source] = block
                value_copy(source, me).start()
        return carry

    lax.fori_loop(0, n // per, answer, 0)

    def prepare(i, carry):
        here = pl.ds(pl.multiple_of(i * CHUNK, CHUNK), CHUNK)
        rank = rank_ref[:, here].astype(jnp.int32)
        hot = one_hot((rank % LANES).astype(F32), LANES)
        hots[:, here] = jnp.concatenate([hot, hot], axis=0)
        return carry

    lax.fori_loop(0, faces // CHUNK, prepare, 0)

    def take_block(t, carry):
        first = lax.rem(mine + blocks - t, blocks) * BLOCK
        lines = []
        for i in range(BLOCK):

            @pl.when(first + i != me)
            def _():
                value_copy(first + i, first + i).wait_recv()

            lines.append(incoming[first + i])
        high, low = split(jnp.concatenate(lines, axis=0))
        held = jnp.concatenate([high.astype(BF16), low.astype(BF16)], axis=1)

        def take_chunk(j, carry):
            here = pl.ds(pl.multiple_of(j * CHUNK, CHUNK), CHUNK)
            picked = jnp.dot(held, hots[:, here], preferred_element_type=F32)
            owner = jnp.broadcast_to(owner_ref[:, here], (deep, CHUNK))
            value = jnp.where(t == 0, 0.0, found[:, here])
            for i in range(BLOCK):
                value = jnp.where(owner == first + i, picked[i * deep : (i + 1) * deep], value)
            found[:, here] = value
            return carry

        lax.fori_loop(0, faces // CHUNK, take_chunk, 0)
        return carry

    found[...] = jnp.zeros_like(found)
    lax.fori_loop(0, blocks, take_block, 0)

    def face(j, carry):
        here = pl.ds(pl.multiple_of(j * CHUNK, CHUNK), CHUNK)
        part = rank_ref[:, here].astype(jnp.int32) // LANES
        node = found[:12, here]
        for h in range(1, halves):
            node = jnp.where(part == h, found[12 * h : 12 * h + 12, here], node)
        faced = exact(spread, node)
        for k in range(NODES_F):
            out_ref[k, :, here] = faced[8 * k : 8 * k + 3]
        return carry

    lax.fori_loop(0, faces // CHUNK, face, 0)

    def finish(k, carry):
        value_copy(lax.rem(me + k, n), me).wait_send()
        return carry

    lax.fori_loop(1, n, finish, 0)


def homeward(cap, disp, number, owner, rank, transfer):
    members = lax.axis_size("dev")
    n = lax.axis_size("grp") * members
    faces = owner.shape[1]
    _, rows, cols = disp.shape
    halves, deep = place_of(cap)
    return pl.pallas_call(
        functools.partial(homeward_kernel, n, members, cap, rows, cols),
        in_specs=[VM] * 5,
        out_specs=VM,
        out_shape=jax.ShapeDtypeStruct((NODES_F, 3, faces), F32),
        scratch_shapes=[
            pltpu.VMEM((12 * rows, 2 * cols), BF16), pltpu.VMEM((2 * LANES, faces), BF16),
            pltpu.VMEM((deep, faces), F32),
            pltpu.VMEM((n, deep, LANES), F32), pltpu.VMEM((n, deep, LANES), F32),
        ] + [pltpu.SemaphoreType.DMA((n,))] * 2,
        compiler_params=pltpu.CompilerParams(
            collective_id=2, has_side_effects=True, vmem_limit_bytes=VMEM_LIMIT),
        name="homeward",
    )(disp, number, owner, rank, transfer)


AROUND = [(1, 0), (-1, 0), (0, 1), (0, -1), (1, 1), (1, -1), (-1, 1), (-1, -1)]


def exchange_kernel(groups, members, rows, edge, strip, edges, strips, corners, send, recv):
    g, d = lax.axis_index("grp"), lax.axis_index("dev")

    def exists(up, right):
        row, col = g + up, d + right
        return (row >= 0) & (row < groups) & (col >= 0) & (col < members)

    barrier = pltpu.get_barrier_semaphore()
    for up, right in AROUND:

        @pl.when(exists(up, right))
        def _():
            pl.semaphore_signal(barrier, inc=1, device_id=(g + up, d + right), device_id_type=MESH)

    one = lambda condition: jnp.where(condition, 1, 0).astype(jnp.int32)
    near_rows = 1 + one(g > 0) + one(g < groups - 1)
    near_cols = 1 + one(d > 0) + one(d < members - 1)
    pl.semaphore_wait(barrier, near_rows * near_cols - 1)

    copies = []
    for k, (up, right) in enumerate(AROUND):
        v, h = (0 if up == 1 else 1), (0 if right == 1 else 1)
        if right == 0:
            source, target = edge.at[1 - v], edges.at[v]
        elif up == 0:
            source, target = strip.at[1 - h], strips.at[h]
        else:
            start = rows - SWEEPS if up == 1 else 0
            source, target = strip.at[1 - h, :, pl.ds(start, SWEEPS), :], corners.at[v, h]
        copy = pltpu.make_async_remote_copy(
            src_ref=source, dst_ref=target, send_sem=send.at[k], recv_sem=recv.at[k],
            device_id=(g + up, d + right), device_id_type=MESH,
        )
        copies.append(copy)
        pl.when(exists(up, right))(copy.start)
    for k, (up, right) in enumerate(AROUND):
        pl.when(exists(up, right))(copies[k].wait_send)
        pl.when(exists(-up, -right))(copies[k].wait_recv)


def exchange(edge, strip, rows):
    groups, members = lax.axis_size("grp"), lax.axis_size("dev")
    shapes = [edge.shape, strip.shape, (2, 2, 2, SWEEPS, LANES)]
    return pl.pallas_call(
        functools.partial(exchange_kernel, groups, members, rows),
        in_specs=[ANY, ANY],
        out_specs=[ANY] * 3,
        out_shape=[jax.ShapeDtypeStruct(s, F32) for s in shapes],
        scratch_shapes=[pltpu.SemaphoreType.DMA((8,)), pltpu.SemaphoreType.DMA((8,))],
        compiler_params=pltpu.CompilerParams(collective_id=0, has_side_effects=True),
        name="exchange",
    )(edge, strip)


def sweep_kernel(rows, cols, prev_ref, load_ref, scale_ref, edge_ref, strip_ref, corner_ref,
                 inverse_ref, flag_ref, out_ref, one, two, base, factor):
    top = 2 * SWEEPS
    wide = cols + LANES
    tall = rows + 2 * top
    zero_rows = jnp.zeros((12, SWEEPS, wide), F32)
    for start in (0, tall - SWEEPS):
        one[:, start : start + SWEEPS, :] = zero_rows
        two[:, start : start + SWEEPS, :] = zero_rows
    one[:, top : top + rows, :cols] = prev_ref[...]
    base[:, top : top + rows, :cols] = load_ref[...]
    factor[top : top + rows, :cols] = scale_ref[...]
    near = [flag_ref[k] > 0 for k in range(4)]
    for side, start in ((0, top - SWEEPS), (1, top + rows)):
        shell = jnp.where(near[side], edge_ref[side], 0.0)
        one[:, start : start + SWEEPS, :cols] = shell[:12]
        base[:, start : start + SWEEPS, :cols] = shell[13:]
        factor[start : start + SWEEPS, :cols] = shell[12]

    def unpack(west, east, start, kind, at_all):
        size = west.shape[0]
        west = jnp.where(near[2] & at_all, west, 0.0)
        east = jnp.where(near[3] & at_all, east, 0.0)
        lane = lax.broadcasted_iota(jnp.int32, (size, LANES), 1)
        for j in range(13 if kind == 0 else 12):
            back = (LANES - j * SWEEPS) % LANES
            first = pltpu.roll(east, back, 1) if back else east
            back = (back - SWEEPS) % LANES
            last = pltpu.roll(west, back, 1) if back else west
            piece = jnp.where(lane < SWEEPS, first, jnp.where(lane >= LANES - SWEEPS, last, 0.0))
            if j == 12:
                factor[start : start + size, cols:] = piece
            elif kind == 0:
                one[j, start : start + size, cols:] = piece
            else:
                base[j, start : start + size, cols:] = piece

    for kind in range(2):
        unpack(strip_ref[0, kind], strip_ref[1, kind], top, kind, near[2] | near[3])
        for side, start in ((0, top - SWEEPS), (1, top + rows)):
            unpack(corner_ref[side, 0, kind], corner_ref[side, 1, kind], start, kind, near[side])

    starts = list(range(top - SWEEPS, top + rows + SWEEPS, 8))
    for start in starts:
        here = slice(start, start + 8)
        scale = factor[here, :]
        inside = scale > 0.0
        inv = jnp.where(inside, 1.0 / jnp.where(inside, scale, 1.0), 0.0)
        loads = [base[j, here, :] for j in range(12)]
        for i in range(12):
            total = inverse_ref[i, 0] * loads[0]
            for j in range(1, 12):
                total = total + inverse_ref[i, j] * loads[j]
            base[i, here, :] = total * inv
        factor[here, :] = inv * coupling_weight

    def relax(source, target, wanted, offset=0):
        for start in wanted:
            here = slice(start, start + 8)
            south = slice(start - 1, start + 7)
            north = slice(start + 1, start + 9)
            sources = []
            for node, (turn, beside, rows_at, below) in enumerate(
                ((1, 1, south, 2), (wide - 1, 0, south, 3), (1, 3, north, 0), (wide - 1, 2, north, 1))
            ):
                for c in range(3):
                    sources.append(
                        pltpu.roll(source[3 * beside + c, here, :], turn, 1)
                        + source[3 * below + c, rows_at, :]
                    )
            inv = factor[here, :]
            for i in range(12):
                total = inverse_ref[i, 0] * sources[0]
                for j in range(1, 12):
                    total = total + inverse_ref[i, j] * sources[j]
                total = base[i, here, :] + total * inv
                target[i, start - offset : start - offset + 8, :] = total[:, : target.shape[2]]

    def pair(_, carry):
        relax(one, two, starts)
        relax(two, one, starts)
        return carry

    lax.fori_loop(0, SWEEPS // 2 - 1, pair, 0)
    relax(one, two, starts)
    relax(two, out_ref, starts[1:-1], top)


def sweep(rows, cols, prev, load, scale, edges, strips, corners, inverse):
    tall, wide = rows + 4 * SWEEPS, cols + LANES
    g, d = lax.axis_index("grp"), lax.axis_index("dev")
    flags = jnp.stack(
        [g > 0, g < lax.axis_size("grp") - 1, d > 0, d < lax.axis_size("dev") - 1]
    ).astype(jnp.int32)
    return pl.pallas_call(
        functools.partial(sweep_kernel, rows, cols),
        in_specs=[VM] * 6 + [SM] * 2,
        out_specs=VM,
        out_shape=jax.ShapeDtypeStruct((12, rows, cols), F32),
        scratch_shapes=[pltpu.VMEM((12, tall, wide), F32)] * 3 + [pltpu.VMEM((tall, wide), F32)],
        name="sweep",
    )(prev, load, scale, edges, strips, corners, inverse, flags)


def local(
    face_owner,
    face_element,
    element_state,
    lift,
    face_scale,
    transfer,
    stiffness_ref,
    element_scale,
    displacement_prev,
):
    n = lax.axis_size("grp") * lax.axis_size("dev")
    faces = face_owner.shape[0]
    cap = -(-(2 * faces // n) // LANES) * LANES
    rows, cols = element_scale.shape
    prev = displacement_prev.reshape(12, rows, cols)
    owner = face_owner.reshape(1, faces)
    load, edge, strip, number, rank, inverse = outward(
        cap, owner, face_element.reshape(1, faces), element_state, lift,
        face_scale.reshape(1, faces), transfer, stiffness_ref, prev, element_scale,
    )
    edges, strips, corners = exchange(edge, strip, rows)
    disp = sweep(rows, cols, prev, load, element_scale, edges, strips, corners, inverse)
    face_displacement = homeward(cap, disp, number, owner, rank, transfer)
    return (disp.reshape(4, 3, rows, cols), face_displacement.transpose(1, 0, 2))


def solution(mesh):
    placed = (
        P(("grp", "dev"), None),
        P(("grp", "dev")),
        P(None, ("grp", "dev")),
        P(),
        P(("grp", "dev")),
        P(),
        P(),
        P("grp", "dev"),
        P(None, None, "grp", "dev"),
    )
    return jax.shard_map(
        local,
        mesh=mesh,
        in_specs=placed,
        out_specs=(P(None, None, "grp", "dev"), P(None, None, ("grp", "dev"))),
        check_vma=False,
    )
```

```python
import functools

import jax
import jax.numpy as jnp
from jax import lax
from jax.experimental import pallas as pl
from jax.experimental.pallas import tpu as pltpu
from jax.sharding import PartitionSpec as P

NODES_F = 10
SWEEPS = 8
LANES = 128
VMEM_LIMIT = 56 * 1024 * 1024

coupling_weight = 2.2
highest = lax.Precision.HIGHEST
F32 = jnp.float32
BF16 = jnp.bfloat16
NT = (((1,), (1,)), ((), ()))
VM = pl.BlockSpec(memory_space=pltpu.VMEM)
SM = pl.BlockSpec(memory_space=pltpu.SMEM)


def split(x):
    high = x.astype(BF16).astype(F32)
    return high, x - high


def one_hot(row, count):
    places = lax.broadcasted_iota(jnp.int32, (count, row.shape[1]), 0).astype(F32)
    return jnp.where(places == row, 1.0, 0.0).astype(BF16)


MESH = pl.DeviceIdType.MESH
ANY = pl.BlockSpec(memory_space=pl.ANY)
BLOCK = 8
COLLECT_FAR = False
SPLIT_PART = 0.5
TAKE_FAR = True
CHUNK = 512


def triple(x):
    high = x.astype(BF16)
    rest = x - high.astype(F32)
    middle = rest.astype(BF16)
    return high, middle, (rest - middle.astype(F32)).astype(BF16)


def exact(a, b, dims=(((1,), (0,)), ((), ()))):
    return lax.dot_general(a, b, dims, precision=highest, preferred_element_type=F32)


def same(shape, of_row, of_col):
    left = of_row(lax.broadcasted_iota(jnp.int32, (shape[0], 1), 0))
    return left == of_col(lax.broadcasted_iota(jnp.int32, (1, shape[1]), 1))


def pick(shape, of_row, of_col):
    return jnp.where(same(shape, of_row, of_col), 1.0, 0.0).astype(F32)


def place_of(cap):
    halves = cap // LANES
    return halves, -(-12 * halves // 8) * 8


def identity_of(t, members):
    return (t // members, lax.rem(t, members))


def partner(me, k, n):
    other, bit = 0, 1
    while bit < n:
        a, b = lax.rem(lax.div(me, bit), 2), lax.rem(lax.div(k, bit), 2)
        other = other + bit * (a + b - 2 * a * b)
        bit *= 2
    return other


def turn_of(m, n, members, far_first):
    half, near = n // 2, members // 2
    part, m = lax.div(m, half), lax.rem(m, half)
    top = 1 - part if far_first else part
    return lax.div(m, near) * members + top * near + lax.rem(m, near)


def greet_all(n, members, me):
    barrier = pltpu.get_barrier_semaphore()

    def greet(k, carry):
        pl.semaphore_signal(
            barrier, inc=1, device_id=identity_of(lax.rem(me + k, n), members), device_id_type=MESH
        )
        return carry

    lax.fori_loop(1, n, greet, 0)
    return barrier


AROUND = [(1, 0), (-1, 0), (0, 1), (0, -1), (1, 1), (1, -1), (-1, 1), (-1, -1)]
HIGH = 16
SIDE = 8


def node_of(t, q):
    return jnp.where(t == 0, q // 3, 3 - q // 3)


def mixing(inverse, levels):
    def lanes_at(shape, axis):
        lane = lax.broadcasted_iota(jnp.int32, shape, axis)
        t, l = lane // LANES, lane % LANES
        return t, l % 6, jnp.where(l < 6 * levels, l // 6, -1 - axis)

    def ones(condition):
        return jnp.where(condition, 1.0, 0.0).astype(F32)

    wide = 2 * LANES
    t, q, target_level = lanes_at((1, wide), 1)
    to = ones(lax.broadcasted_iota(jnp.int32, (12, wide), 0) == 3 * node_of(t, q) + q % 3)
    t, q, level = lanes_at((wide, 1), 0)
    source = 3 * jnp.where(t == 0, 1 - q // 3, 2 + q // 3) + q % 3
    out = ones(lax.broadcasted_iota(jnp.int32, (wide, 12), 1) == source)
    couple = exact(exact(out, inverse, NT), to) * coupling_weight
    return jnp.where(level == target_level, couple, 0.0)


def stacked(matrix):
    high = matrix.astype(BF16)
    low = (matrix - high.astype(F32)).astype(BF16)
    return jnp.concatenate([high, high, low], axis=0)


def times(x, held):
    high = x.astype(BF16)
    low = (x - high.astype(F32)).astype(BF16)
    return jnp.dot(jnp.concatenate([high, low, high], axis=1), held, preferred_element_type=F32)


def step_kernel(n, groups, members, cap, rows, cols, owner_ref, element_ref, state_ref, lift_ref,
                   scale_ref, transfer_ref, stiff_ref, prev_ref, factor_ref,
                   disp_ref, out_ref,
                   highs, lows, hots, outgoing, incoming, number_out, number_in, rank_ref,
                   shell, other, base, turned, strides, total_load, total_edge, total_inner,
                   couple_held, early, early_in, early_corner, late, late_in, late_corner,
                   table, lane_hots, found, answers, answered,
                   send, recv, number_send, number_recv, near_send, near_recv, back_send, back_recv):
    g, d = lax.axis_index("grp"), lax.axis_index("dev")
    me = g * members + d
    faces = owner_ref.shape[1]
    halves, deep = place_of(cap)
    layers = rows // HIGH
    halo = SWEEPS // layers
    levels = HIGH + 2 * halo
    run = 6 * halo
    first_col = 2 * SIDE
    inner = slice(first_col, first_col + cols)

    shell[...] = jnp.zeros_like(shell)
    base[...] = jnp.zeros_like(base)
    other[...] = jnp.zeros_like(other)
    turned[...] = jnp.zeros_like(turned)
    barrier = greet_all(n, members, me)

    def component(t, q):
        return 3 * (q // 3 if t == 0 else 3 - q // 3) + q % 3

    lane_tiles = [slice(w * LANES, (w + 1) * LANES) for w in range(cols // LANES)]
    for w, tile in enumerate(lane_tiles):
        strides[w, :12] = prev_ref[:, :, tile]
        strides[w, 12] = 1.0 / factor_ref[:, tile]
    for k in range(layers):
        for t in range(3):
            for w in range(len(lane_tiles)):
                for q in range(6):
                    turned[k * 3 + t, w, pl.ds(run + q, HIGH, stride=6), :] = (
                        strides[w, component(t, q) if t < 2 else 12, pl.ds(k, HIGH, stride=layers), :])
                shell[k, first_col + w * LANES : first_col + (w + 1) * LANES,
                      t * LANES : (t + 1) * LANES] = turned[k * 3 + t, w].T

    stiffness = stiff_ref[...]
    identity = pick((12, 12), lambda i: i, lambda j: j)
    approx = identity / 5.0
    rest = identity - stiffness / 5.0
    for _ in range(8):
        both = exact(jnp.concatenate([approx, rest], axis=0), rest)
        approx, rest = approx + both[:12], both[12:]
    couple_held[...] = stacked(mixing(approx, levels))

    spread = exact(exact(pick((16, 4), lambda i: i // 3, lambda j: j), transfer_ref[...]),
                   pick((NODES_F, 3 * NODES_F), lambda i: i, lambda j: j % NODES_F))
    kept = same(spread.shape, lambda i: i % 3, lambda j: j // NODES_F)
    kept = kept & (lax.broadcasted_iota(jnp.int32, spread.shape, 0) < 12)
    spread = jnp.where(kept, spread, 0.0)[:12]
    spread = jnp.concatenate([exact(approx, spread), jnp.zeros((4, spread.shape[1]), F32)], axis=0)
    gather = jnp.concatenate(triple(exact(spread, lift_ref[...].astype(F32))), axis=0)
    before = jnp.where(
        lax.broadcasted_iota(jnp.int32, (CHUNK, CHUNK), 0)
        < lax.broadcasted_iota(jnp.int32, (CHUNK, CHUNK), 1), 1.0, 0.0
    ).astype(BF16)

    lane = lax.broadcasted_iota(jnp.int32, (1, LANES), 1)

    def lanes_in(start, size):
        return (lane >= start) & (lane < start + size)

    first_half = lax.rem(lane, 6) < 3

    def slot_of(k, t):
        return run * (2 * k + t if t < 2 else 2 * layers + k // 2)

    def pack(ref, tiles, target):
        for v in range(2):
            start = run if v == 1 else 6 * HIGH
            packed = jnp.zeros((cols, LANES), F32)
            for k in range(layers):
                for t in range(tiles):
                    move = slot_of(k, t)
                    turn = (move - start) % LANES
                    piece = ref[k, inner, t * LANES : (t + 1) * LANES]
                    piece = pltpu.roll(piece, turn, 1) if turn else piece
                    wanted = lanes_in(move, run)
                    if t == 2:
                        wanted = wanted & (first_half == (k % 2 == 0))
                    packed = jnp.where(wanted, piece, packed)
            target[v] = packed

    def unpack(ref, tiles, v, arrived, start, size):
        goal = 0 if v == 0 else run + 6 * HIGH
        keep = lanes_in(goal, run)
        for k in range(layers):
            for t in range(tiles):
                turn = (goal - slot_of(k, t)) % LANES
                piece = pltpu.roll(arrived, turn, 1) if turn else arrived
                if t == 2:
                    piece = jnp.where(first_half == (k % 2 == 0), piece,
                                      pltpu.roll(piece, 3 if k % 2 == 0 else LANES - 3, 1))
                here = slice(start, start + size)
                there = slice(t * LANES, (t + 1) * LANES)
                ref[k, here, there] = jnp.where(keep, piece, ref[k, here, there])

    def exists(up, right):
        row, col = g + up, d + right
        return (row >= 0) & (row < groups) & (col >= 0) & (col < members)

    def neighbour_copies(ref, packed, arrived, corner, number):
        copies = []
        for k, (up, right) in enumerate(AROUND):
            v, h = (0 if up == 1 else 1), (0 if right == 1 else 1)
            if right == 0:
                source, target = packed.at[v], arrived.at[v]
            elif up == 0:
                start, end = (cols + SIDE, SIDE) if right == 1 else (first_col, cols + first_col)
                source, target = ref.at[:, pl.ds(start, SIDE), :], ref.at[:, pl.ds(end, SIDE), :]
            else:
                start = cols - SIDE if right == 1 else 0
                source, target = packed.at[v, pl.ds(start, SIDE), :], corner.at[v, h]
            copies.append(pltpu.make_async_remote_copy(
                src_ref=source, dst_ref=target, send_sem=near_send.at[number, k],
                recv_sem=near_recv.at[number, k],
                device_id=(g + up, d + right), device_id_type=MESH))
        return copies

    def begin(copies, kinds):
        for k, (up, right) in enumerate(AROUND):
            if (up == 0) in kinds:
                pl.when(exists(up, right))(copies[k].start)

    def end(copies, ref, tiles, arrived, corner):
        for k, (up, right) in enumerate(AROUND):
            pl.when(exists(up, right))(copies[k].wait_send)
        for v in range(2):

            @pl.when(exists(2 * v - 1, 0))
            def _():
                copies[v].wait_recv()
                unpack(ref, tiles, v, arrived[v], first_col, cols)

        for k, (up, right) in enumerate(AROUND):
            if right != 0:
                pl.when(exists(-up, -right))(copies[k].wait_recv)
        for v in range(2):
            for h in range(2):

                @pl.when(exists(2 * v - 1, 2 * h - 1))
                def _():
                    unpack(ref, tiles, v, corner[v, h], SIDE if h == 0 else cols + first_col, SIDE)

    pack(shell, 3, early)
    pl.semaphore_wait(barrier, n - 1)
    early_copies = neighbour_copies(shell, early, early_in, early_corner, 0)
    begin(early_copies, (True, False))

    counts = jnp.zeros((n, 1), F32)
    for i in range(faces // CHUNK):
        here = slice(i * CHUNK, (i + 1) * CHUNK)
        owner_hot = one_hot(owner_ref[:, here].astype(F32), n)
        hot = owner_hot.astype(F32)
        running = jnp.dot(owner_hot, before, preferred_element_type=F32) + counts
        counts = counts + jnp.sum(hot, axis=1, keepdims=True)
        rank = jnp.sum(hot * running, axis=0, keepdims=True)
        rank_ref[:, here] = rank
        hots[:, here] = one_hot(rank, cap)
        parts = jnp.dot(gather, state_ref[:, here], preferred_element_type=F32)
        loads = (parts[:16] + parts[16:32] + parts[32:]) * scale_ref[:, here]
        element = element_ref[:, here]
        high_row = (element // cols).astype(F32)
        low_row = (element % cols).astype(F32)
        where_row = lax.broadcasted_iota(jnp.int32, loads.shape, 0)
        values = jnp.where(where_row == 12, high_row, jnp.where(where_row == 13, low_row, loads))
        high, low = split(values)
        highs[:, here] = high
        lows[:, here] = low
    def value_copy(owner, slot):
        return pltpu.make_async_remote_copy(
            src_ref=outgoing.at[owner], dst_ref=incoming.at[slot], send_sem=send.at[owner],
            recv_sem=recv.at[slot], device_id=identity_of(owner, members), device_id_type=MESH)

    def number_copy(owner, slot):
        return pltpu.make_async_remote_copy(
            src_ref=number_out.at[owner], dst_ref=number_in.at[slot], send_sem=number_send.at[owner],
            recv_sem=number_recv.at[slot], device_id=identity_of(owner, members), device_id_type=MESH)

    blocks = n // BLOCK

    def send_block(t, carry):
        owners = [partner(me, turn_of(t * BLOCK + i, n, members, True), n) for i in range(BLOCK)]
        owner_wide = jnp.broadcast_to(owner_ref[...], (16, faces))
        high, low = highs[...], lows[...]
        pieces = []
        for i in range(BLOCK):
            here = owner_wide == owners[i]
            pieces.append(jnp.where(here, high, 0.0).astype(BF16))
            pieces.append(jnp.where(here, low, 0.0).astype(BF16))
        total = lax.dot_general(
            jnp.concatenate(pieces, axis=0), hots[...], NT, preferred_element_type=F32
        )
        for i in range(BLOCK):
            owner = owners[i]
            block = total[32 * i : 32 * i + 16] + total[32 * i + 16 : 32 * i + 32]
            number = (block[12:13] * cols + block[13:14]).astype(jnp.int32)
            lines = [block[:12, h * LANES : (h + 1) * LANES] for h in range(halves)]
            if deep > 12 * halves:
                lines.append(jnp.zeros((deep - 12 * halves, LANES), F32))
            block = jnp.concatenate(lines, axis=0)

            @pl.when(owner == me)
            def _():
                incoming[me] = block
                number_in[me] = number

            @pl.when(owner != me)
            def _():
                outgoing[owner] = block
                number_out[owner] = number
                number_copy(owner, me).start()
                value_copy(owner, me).start()
        return carry

    lax.fori_loop(0, blocks, send_block, 0)
    total_load[...] = jnp.zeros_like(total_load)
    total_edge[...] = jnp.zeros_like(total_edge)
    total_inner[...] = jnp.zeros_like(total_inner)

    per = max(1, min(BLOCK, 1024 // cap))
    width = per * cap

    edge_rows, inner_rows = 12 * 2 * SWEEPS, 12 * (rows - 2 * SWEEPS)

    def level_rows(size, level):
        row = lax.broadcasted_iota(jnp.int32, (size, 1), 0) // 6
        return level(row) * layers

    edge_row = level_rows(2 * run, lambda i: jnp.where(i < halo, i, i + HIGH - 2 * halo))
    inner_row = level_rows(6 * HIGH - 2 * run, lambda i: i + halo)

    def take_sources(t, wait, with_edge, with_inner):
        sources = [partner(me, turn_of(t * per + i, n, members, COLLECT_FAR), n) for i in range(per)]
        if wait:
            for source in sources:

                @pl.when(source != me)
                def _():
                    number_copy(source, source).wait_recv()
                    value_copy(source, source).wait_recv()

        numbers, values = [], []
        for source in sources:
            numbers.append(number_in[source])
            value = incoming[source]
            for h in range(halves):
                values.append(value[12 * h : 12 * h + 12])
        number = jnp.concatenate(numbers, axis=1)
        value = jnp.concatenate(values, axis=1)
        row = number // cols
        low_hot = one_hot((number % cols).astype(F32), cols)
        lefts = []
        for part in split(value):
            tiles = [
                jnp.concatenate([part[component(t, 0) : component(t, 0) + 3],
                                 part[component(t, 3) : component(t, 3) + 3]] * 4, axis=0)
                for t in range(2)
            ]
            pieces = []
            for wanted, level in ((with_edge, edge_row), (with_inner, inner_row)):
                if wanted:
                    for k in range(layers):
                        mask = level + k == row
                        for t in range(2):
                            held = [tiles[t]] * (level.shape[0] // 24)
                            held = jnp.concatenate(held, axis=0) if len(held) > 1 else held[0]
                            pieces.append(jnp.where(mask, held, 0.0))
            lefts.append(jnp.concatenate(pieces, axis=0).astype(BF16))
        left = jnp.concatenate(lefts, axis=1)
        right = jnp.concatenate([low_hot, low_hot], axis=1)
        return lax.dot_general(right, left, NT, preferred_element_type=F32)

    def take_all(t, carry):
        total_load[...] += take_sources(t, True, True, True)
        return carry

    def take_edge(t, carry):
        total_edge[...] += take_sources(t, True, True, False)
        return carry

    def take_inner(t, carry):
        total_inner[...] += take_sources(t, False, False, True)
        return carry

    def placed(value, start, size, target):
        result = None
        for tile in range(start // LANES, (start + size - 1) // LANES + 1):
            end = min((tile + 1) * LANES, value.shape[1])
            piece = value[:, tile * LANES : end]
            if end < (tile + 1) * LANES:
                piece = jnp.concatenate([piece, jnp.zeros((cols, (tile + 1) * LANES - end), F32)], axis=1)
            turn = (target - start) % LANES
            piece = pltpu.roll(piece, turn, 1) if turn else piece
            first, last = max(start, tile * LANES), min(start + size, (tile + 1) * LANES)
            wanted = lanes_in(target + first - start, last - first)
            result = jnp.where(wanted, piece, 0.0 if result is None else result)
        return result

    steps = n // per
    split_at = steps - int(steps * SPLIT_PART)
    lax.fori_loop(0, split_at, take_all, 0)
    end(early_copies, shell, 3, early_in, early_corner)
    lax.fori_loop(split_at, steps, take_edge, 0)
    edge_total = total_load[:, :edge_rows] + total_edge[...]
    for k in range(layers):
        inv = shell[k, inner, 2 * LANES :]
        for t in range(2):
            start = (2 * k + t) * 2 * run
            value = placed(edge_total, start, run, run) + placed(edge_total, start + run, run, 6 * HIGH)
            base[k, inner, t * LANES : (t + 1) * LANES] = value * inv
    pack(base, 2, late)
    late_copies = neighbour_copies(base, late, late_in, late_corner, 1)
    begin(late_copies, (False,))
    lax.fori_loop(split_at, steps, take_inner, 0)
    inner_total = total_load[:, edge_rows:] + total_inner[...]
    for k in range(layers):
        inv = shell[k, inner, 2 * LANES :]
        for t in range(2):
            size = 6 * HIGH - 2 * run
            value = placed(inner_total, (2 * k + t) * size, size, 2 * run)
            there = slice(t * LANES, (t + 1) * LANES)
            base[k, inner, there] = base[k, inner, there] + value * inv
    begin(late_copies, (True,))
    end(late_copies, base, 2, late_in, late_corner)

    all_cols = cols + first_col
    here, east, west = (pl.ds(SIDE + move, all_cols) for move in (0, 1, -1))

    def relax(source, target):
        for k in range(layers):
            if k > 0:
                south = source[k - 1, here, LANES : 2 * LANES]
            else:
                south = pltpu.roll(source[layers - 1, here, LANES : 2 * LANES], 6, 1)
            if k < layers - 1:
                north = source[k + 1, here, :LANES]
            else:
                north = pltpu.roll(source[0, here, :LANES], LANES - 6, 1)
            first = jnp.where(first_half, source[k, east, :LANES], source[k, west, :LANES]) + south
            second = jnp.where(
                first_half, source[k, west, LANES : 2 * LANES], source[k, east, LANES : 2 * LANES]
            ) + north
            moved = times(jnp.concatenate([first, second], axis=1), couple_held[...])
            inv = shell[k, here, 2 * LANES :]
            target[k, here, : 2 * LANES] = base[k, here, :] + moved * jnp.concatenate([inv, inv], axis=1)

    def pair(_, carry):
        relax(shell, other)
        relax(other, shell)
        return carry

    lax.fori_loop(0, SWEEPS // 2, pair, 0)

    for k in range(layers):
        for t in range(2):
            for w in range(len(lane_tiles)):
                turned[k * 3 + t, w] = shell[k, first_col + w * LANES : first_col + (w + 1) * LANES,
                                             t * LANES : (t + 1) * LANES].T
                for q in range(6):
                    strides[w, component(t, q), pl.ds(k, HIGH, stride=layers), :] = (
                        turned[k * 3 + t, w, pl.ds(run + q, HIGH, stride=6), :])
    for w, tile in enumerate(lane_tiles):
        value = strides[w, :12]
        disp_ref[:, :, tile] = value
        high, low = split(value.reshape(12 * rows, LANES))
        table[:, tile] = high.astype(BF16)
        table[:, cols + w * LANES : cols + (w + 1) * LANES] = low.astype(BF16)

    spread = exact(
        pick((8 * NODES_F, NODES_F), lambda i: i // 8, lambda j: j),
        exact(transfer_ref[...], pick((4, 12), lambda i: i, lambda j: j // 3), (((0,), (0,)), ((), ()))),
    )
    spread = jnp.where(same(spread.shape, lambda i: i % 8, lambda j: j % 3), spread, 0.0)

    def back_copy(owner, slot):
        return pltpu.make_async_remote_copy(
            src_ref=answers.at[owner], dst_ref=answered.at[slot], send_sem=back_send.at[owner],
            recv_sem=back_recv.at[slot], device_id=identity_of(owner, members), device_id_type=MESH)

    def answer(t, carry):
        sources = [partner(me, turn_of(t * per + i, n, members, True), n) for i in range(per)]
        number = jnp.concatenate([number_in[source] for source in sources], axis=1)
        mask = lax.broadcasted_iota(jnp.int32, (rows, width), 0) == number // cols
        low_hot = one_hot((number % cols).astype(F32), cols)
        picked = jnp.dot(
            table[...], jnp.concatenate([low_hot, low_hot], axis=0), preferred_element_type=F32
        )
        lines = [
            jnp.sum(jnp.where(mask, picked[c * rows : (c + 1) * rows], 0.0), axis=0, keepdims=True)
            for c in range(12)
        ]
        result = jnp.concatenate(lines, axis=0)
        for i, source in enumerate(sources):
            parts = [
                result[:, i * cap + h * LANES : i * cap + (h + 1) * LANES] for h in range(halves)
            ]
            if deep > 12 * halves:
                parts.append(jnp.zeros((deep - 12 * halves, LANES), F32))
            block = jnp.concatenate(parts, axis=0)

            @pl.when(source == me)
            def _():
                answered[me] = block

            @pl.when(source != me)
            def _():
                answers[source] = block
                back_copy(source, me).start()
        return carry

    lax.fori_loop(0, n // per, answer, 0)

    def prepare(i, carry):
        here = pl.ds(pl.multiple_of(i * CHUNK, CHUNK), CHUNK)
        rank = rank_ref[:, here].astype(jnp.int32)
        hot = one_hot((rank % LANES).astype(F32), LANES)
        lane_hots[:, here] = jnp.concatenate([hot, hot], axis=0)
        return carry

    lax.fori_loop(0, faces // CHUNK, prepare, 0)

    def take_block(t, carry):
        sources = [partner(me, turn_of(t * BLOCK + i, n, members, TAKE_FAR), n) for i in range(BLOCK)]
        lines = []
        for source in sources:

            @pl.when(source != me)
            def _():
                back_copy(source, source).wait_recv()

            lines.append(answered[source])
        high, low = split(jnp.concatenate(lines, axis=0))
        held = jnp.concatenate([high.astype(BF16), low.astype(BF16)], axis=1)

        for j in range(faces // CHUNK):
            here = slice(j * CHUNK, (j + 1) * CHUNK)
            picked = jnp.dot(held, lane_hots[:, here], preferred_element_type=F32)
            owner = jnp.broadcast_to(owner_ref[:, here], (deep, CHUNK))
            value = found[:, here]
            for i in range(BLOCK):
                value = jnp.where(owner == sources[i], picked[i * deep : (i + 1) * deep], value)
            found[:, here] = value
        return carry

    found[...] = jnp.zeros_like(found)
    lax.fori_loop(0, blocks, take_block, 0)

    high = spread.astype(BF16)
    low = (spread - high.astype(F32)).astype(BF16)
    held = jnp.concatenate([high, high, low], axis=1)
    for j in range(faces // CHUNK):
        here = slice(j * CHUNK, (j + 1) * CHUNK)
        part = rank_ref[:, here].astype(jnp.int32) // LANES
        node = found[:12, here]
        for h in range(1, halves):
            node = jnp.where(part == h, found[12 * h : 12 * h + 12, here], node)
        high = node.astype(BF16)
        low = (node - high.astype(F32)).astype(BF16)
        faced = jnp.dot(
            held, jnp.concatenate([high, low, high], axis=0), preferred_element_type=F32
        )
        for k in range(NODES_F):
            out_ref[k, :, here] = faced[8 * k : 8 * k + 3]

    def finish(k, carry):
        owner = lax.rem(me + k, n)
        number_copy(owner, me).wait_send()
        value_copy(owner, me).wait_send()
        back_copy(owner, me).wait_send()
        return carry

    lax.fori_loop(1, n, finish, 0)


def outward(cap, owner, element, state, lift, scale, transfer, stiffness, prev, factor):
    groups, members = lax.axis_size("grp"), lax.axis_size("dev")
    n = groups * members
    faces = owner.shape[1]
    _, rows, cols = prev.shape
    halves, deep = place_of(cap)
    layers = rows // HIGH
    tall = cols + 4 * SIDE
    near = [pltpu.VMEM((2, cols, LANES), F32), pltpu.VMEM((2, cols, LANES), F32),
            pltpu.VMEM((2, 2, SIDE, LANES), F32)]
    return pl.pallas_call(
        functools.partial(step_kernel, n, groups, members, cap, rows, cols),
        in_specs=[VM] * 9,
        out_specs=[VM] * 2,
        out_shape=[jax.ShapeDtypeStruct((12, rows, cols), F32),
                   jax.ShapeDtypeStruct((NODES_F, 3, faces), F32)],
        scratch_shapes=[
            pltpu.VMEM((16, faces), F32), pltpu.VMEM((16, faces), F32), pltpu.VMEM((cap, faces), BF16),
            pltpu.VMEM((n, deep, LANES), F32), pltpu.VMEM((n, deep, LANES), F32),
            pltpu.VMEM((n, 1, cap), jnp.int32), pltpu.VMEM((n, 1, cap), jnp.int32),
            pltpu.VMEM((1, faces), F32),
            pltpu.VMEM((layers, tall, 3 * LANES), F32), pltpu.VMEM((layers, tall, 2 * LANES), F32),
            pltpu.VMEM((layers, tall, 2 * LANES), F32), pltpu.VMEM((3 * layers, cols // LANES, LANES, LANES), F32),
            pltpu.VMEM((cols // LANES, 13, rows, LANES), F32), pltpu.VMEM((cols, 12 * rows), F32),
            pltpu.VMEM((cols, 24 * SWEEPS), F32), pltpu.VMEM((cols, 12 * rows - 24 * SWEEPS), F32),
            pltpu.VMEM((6 * LANES, 2 * LANES), BF16),
        ] + near + near + [
            pltpu.VMEM((12 * rows, 2 * cols), BF16), pltpu.VMEM((2 * LANES, faces), BF16),
            pltpu.VMEM((deep, faces), F32),
            pltpu.VMEM((n, deep, LANES), F32), pltpu.VMEM((n, deep, LANES), F32),
        ] + [pltpu.SemaphoreType.DMA((n,))] * 4 + [pltpu.SemaphoreType.DMA((2, 8))] * 2
        + [pltpu.SemaphoreType.DMA((n,))] * 2,
        compiler_params=pltpu.CompilerParams(
            collective_id=1, has_side_effects=True, vmem_limit_bytes=VMEM_LIMIT),
        name="step",
    )(owner, element, state, lift, scale, transfer, stiffness, prev, factor)


def local(
    face_owner,
    face_element,
    element_state,
    lift,
    face_scale,
    transfer,
    stiffness_ref,
    element_scale,
    displacement_prev,
):
    n = lax.axis_size("grp") * lax.axis_size("dev")
    faces = face_owner.shape[0]
    cap = -(-(2 * faces // n) // LANES) * LANES
    rows, cols = element_scale.shape
    prev = displacement_prev.reshape(12, rows, cols)
    owner = face_owner.reshape(1, faces)
    disp, face_displacement = outward(
        cap, owner, face_element.reshape(1, faces), element_state, lift,
        face_scale.reshape(1, faces), transfer, stiffness_ref, prev, element_scale,
    )
    return (disp.reshape(4, 3, rows, cols), face_displacement.transpose(1, 0, 2))


def solution(mesh):
    placed = (
        P(("grp", "dev"), None),
        P(("grp", "dev")),
        P(None, ("grp", "dev")),
        P(),
        P(("grp", "dev")),
        P(),
        P(),
        P("grp", "dev"),
        P(None, None, "grp", "dev"),
    )
    return jax.shard_map(
        local,
        mesh=mesh,
        in_specs=placed,
        out_specs=(P(None, None, "grp", "dev"), P(None, None, ("grp", "dev"))),
        check_vma=False,
    )
```

```python
import functools

import jax
import jax.numpy as jnp
from jax import lax
from jax.experimental import pallas as pl
from jax.experimental.pallas import tpu as pltpu
from jax.sharding import PartitionSpec as P

NODES_F = 10
SWEEPS = 8
LANES = 128
VMEM_LIMIT = 56 * 1024 * 1024

coupling_weight = 2.2
highest = lax.Precision.HIGHEST
F32 = jnp.float32
BF16 = jnp.bfloat16
NT = (((1,), (1,)), ((), ()))
VM = pl.BlockSpec(memory_space=pltpu.VMEM)
SM = pl.BlockSpec(memory_space=pltpu.SMEM)


def split(x):
    high = x.astype(BF16).astype(F32)
    return high, x - high


def one_hot(row, count):
    places = lax.broadcasted_iota(jnp.int32, (count, row.shape[1]), 0).astype(F32)
    return jnp.where(places == row, 1.0, 0.0).astype(BF16)


MESH = pl.DeviceIdType.MESH
ANY = pl.BlockSpec(memory_space=pl.ANY)
BLOCK = 8
COLLECT_FAR = False
SPLIT_PART = 0.75
TAKE_FAR = True
CHUNK = 512


def triple(x):
    high = x.astype(BF16)
    rest = x - high.astype(F32)
    middle = rest.astype(BF16)
    return high, middle, (rest - middle.astype(F32)).astype(BF16)


def exact(a, b, dims=(((1,), (0,)), ((), ()))):
    return lax.dot_general(a, b, dims, precision=highest, preferred_element_type=F32)


def same(shape, of_row, of_col):
    left = of_row(lax.broadcasted_iota(jnp.int32, (shape[0], 1), 0))
    return left == of_col(lax.broadcasted_iota(jnp.int32, (1, shape[1]), 1))


def pick(shape, of_row, of_col):
    return jnp.where(same(shape, of_row, of_col), 1.0, 0.0).astype(F32)


def place_of(cap):
    halves = cap // LANES
    return halves, -(-12 * halves // 8) * 8


def identity_of(t, members):
    return (t // members, lax.rem(t, members))


def partner(me, k, n):
    other, bit = 0, 1
    while bit < n:
        a, b = lax.rem(lax.div(me, bit), 2), lax.rem(lax.div(k, bit), 2)
        other = other + bit * (a + b - 2 * a * b)
        bit *= 2
    return other


def turn_of(m, n, members, far_first):
    half, near = n // 2, members // 2
    part, m = lax.div(m, half), lax.rem(m, half)
    top = 1 - part if far_first else part
    row, rows_of = lax.div(m, near) * 2, n // members
    row = lax.rem(row, rows_of) + lax.div(row, rows_of)
    return row * members + top * near + lax.rem(m, near)


def greet_all(n, members, me):
    barrier = pltpu.get_barrier_semaphore()

    def greet(k, carry):
        pl.semaphore_signal(
            barrier, inc=1, device_id=identity_of(lax.rem(me + k, n), members), device_id_type=MESH
        )
        return carry

    lax.fori_loop(1, n, greet, 0)
    return barrier


AROUND = [(1, 0), (-1, 0), (0, 1), (0, -1), (1, 1), (1, -1), (-1, 1), (-1, -1)]
HIGH = 16
SIDE = 8


def node_of(t, q):
    return jnp.where(t == 0, q // 3, 3 - q // 3)


def mixing(inverse, levels):
    def lanes_at(shape, axis):
        lane = lax.broadcasted_iota(jnp.int32, shape, axis)
        t, l = lane // LANES, lane % LANES
        return t, l % 6, jnp.where(l < 6 * levels, l // 6, -1 - axis)

    def ones(condition):
        return jnp.where(condition, 1.0, 0.0).astype(F32)

    wide = 2 * LANES
    t, q, target_level = lanes_at((1, wide), 1)
    to = ones(lax.broadcasted_iota(jnp.int32, (12, wide), 0) == 3 * node_of(t, q) + q % 3)
    t, q, level = lanes_at((wide, 1), 0)
    source = 3 * jnp.where(t == 0, 1 - q // 3, 2 + q // 3) + q % 3
    out = ones(lax.broadcasted_iota(jnp.int32, (wide, 12), 1) == source)
    couple = exact(exact(out, inverse, NT), to) * coupling_weight
    return jnp.where(level == target_level, couple, 0.0)


def stacked(matrix):
    high = matrix.astype(BF16)
    low = (matrix - high.astype(F32)).astype(BF16)
    return jnp.concatenate([high, high, low], axis=0)


def times(x, held):
    high = x.astype(BF16)
    low = (x - high.astype(F32)).astype(BF16)
    return jnp.dot(jnp.concatenate([high, low, high], axis=1), held, preferred_element_type=F32)


def step_kernel(n, groups, members, cap, rows, cols, owner_ref, element_ref, state_ref, lift_ref,
                   scale_ref, transfer_ref, stiff_ref, prev_ref, factor_ref,
                   disp_ref, out_ref,
                   highs, lows, hots, outgoing, incoming, number_out, number_in, rank_ref,
                   shell, other, base, turned, strides, total_load, total_edge, total_inner,
                   couple_held, early, early_in, early_corner, late, late_in, late_corner,
                   table, lane_hots, found, answers, answered,
                   send, recv, number_send, number_recv, near_send, near_recv, back_send, back_recv, disp_held, disp_sem):
    g, d = lax.axis_index("grp"), lax.axis_index("dev")
    me = g * members + d
    faces = owner_ref.shape[1]
    halves, deep = place_of(cap)
    layers = rows // HIGH
    halo = SWEEPS // layers
    levels = HIGH + 2 * halo
    run = 6 * halo
    first_col = 2 * SIDE
    inner = slice(first_col, first_col + cols)

    shell[...] = jnp.zeros_like(shell)
    base[...] = jnp.zeros_like(base)
    other[...] = jnp.zeros_like(other)
    turned[...] = jnp.zeros_like(turned)
    barrier = greet_all(n, members, me)

    def component(t, q):
        return 3 * (q // 3 if t == 0 else 3 - q // 3) + q % 3

    lane_tiles = [slice(w * LANES, (w + 1) * LANES) for w in range(cols // LANES)]
    for w, tile in enumerate(lane_tiles):
        strides[w, :12] = prev_ref[:, :, tile]
        strides[w, 12] = 1.0 / factor_ref[:, tile]
    for k in range(layers):
        for t in range(3):
            for w in range(len(lane_tiles)):
                for q in range(6):
                    turned[k * 3 + t, w, pl.ds(run + q, HIGH, stride=6), :] = (
                        strides[w, component(t, q) if t < 2 else 12, pl.ds(k, HIGH, stride=layers), :])
                shell[k, first_col + w * LANES : first_col + (w + 1) * LANES,
                      t * LANES : (t + 1) * LANES] = turned[k * 3 + t, w].T

    stiffness = stiff_ref[...]
    identity = pick((12, 12), lambda i: i, lambda j: j)
    approx = identity / 5.0
    rest = identity - stiffness / 5.0
    for _ in range(8):
        both = exact(jnp.concatenate([approx, rest], axis=0), rest)
        approx, rest = approx + both[:12], both[12:]
    couple_held[...] = stacked(mixing(approx, levels))

    spread = exact(exact(pick((16, 4), lambda i: i // 3, lambda j: j), transfer_ref[...]),
                   pick((NODES_F, 3 * NODES_F), lambda i: i, lambda j: j % NODES_F))
    kept = same(spread.shape, lambda i: i % 3, lambda j: j // NODES_F)
    kept = kept & (lax.broadcasted_iota(jnp.int32, spread.shape, 0) < 12)
    spread = jnp.where(kept, spread, 0.0)[:12]
    spread = jnp.concatenate([exact(approx, spread), jnp.zeros((4, spread.shape[1]), F32)], axis=0)
    gather = jnp.concatenate(triple(exact(spread, lift_ref[...].astype(F32))), axis=0)
    before = jnp.where(
        lax.broadcasted_iota(jnp.int32, (CHUNK, CHUNK), 0)
        < lax.broadcasted_iota(jnp.int32, (CHUNK, CHUNK), 1), 1.0, 0.0
    ).astype(BF16)

    lane = lax.broadcasted_iota(jnp.int32, (1, LANES), 1)

    def lanes_in(start, size):
        return (lane >= start) & (lane < start + size)

    first_half = lax.rem(lane, 6) < 3

    def slot_of(k, t):
        return run * (2 * k + t if t < 2 else 2 * layers + k // 2)

    def pack(ref, tiles, target):
        for v in range(2):
            start = run if v == 1 else 6 * HIGH
            packed = jnp.zeros((cols, LANES), F32)
            for k in range(layers):
                for t in range(tiles):
                    move = slot_of(k, t)
                    turn = (move - start) % LANES
                    piece = ref[k, inner, t * LANES : (t + 1) * LANES]
                    piece = pltpu.roll(piece, turn, 1) if turn else piece
                    wanted = lanes_in(move, run)
                    if t == 2:
                        wanted = wanted & (first_half == (k % 2 == 0))
                    packed = jnp.where(wanted, piece, packed)
            target[v] = packed

    def unpack(ref, tiles, v, arrived, start, size):
        goal = 0 if v == 0 else run + 6 * HIGH
        keep = lanes_in(goal, run)
        for k in range(layers):
            for t in range(tiles):
                turn = (goal - slot_of(k, t)) % LANES
                piece = pltpu.roll(arrived, turn, 1) if turn else arrived
                if t == 2:
                    piece = jnp.where(first_half == (k % 2 == 0), piece,
                                      pltpu.roll(piece, 3 if k % 2 == 0 else LANES - 3, 1))
                here = slice(start, start + size)
                there = slice(t * LANES, (t + 1) * LANES)
                ref[k, here, there] = jnp.where(keep, piece, ref[k, here, there])

    def exists(up, right):
        row, col = g + up, d + right
        return (row >= 0) & (row < groups) & (col >= 0) & (col < members)

    def neighbour_copies(ref, packed, arrived, corner, number):
        copies = []
        for k, (up, right) in enumerate(AROUND):
            v, h = (0 if up == 1 else 1), (0 if right == 1 else 1)
            if right == 0:
                source, target = packed.at[v], arrived.at[v]
            elif up == 0:
                start, end = (cols + SIDE, SIDE) if right == 1 else (first_col, cols + first_col)
                source, target = ref.at[:, pl.ds(start, SIDE), :], ref.at[:, pl.ds(end, SIDE), :]
            else:
                start = cols - SIDE if right == 1 else 0
                source, target = packed.at[v, pl.ds(start, SIDE), :], corner.at[v, h]
            copies.append(pltpu.make_async_remote_copy(
                src_ref=source, dst_ref=target, send_sem=near_send.at[number, k],
                recv_sem=near_recv.at[number, k],
                device_id=(g + up, d + right), device_id_type=MESH))
        return copies

    def begin(copies, kinds):
        for k, (up, right) in enumerate(AROUND):
            if (up == 0) in kinds:
                pl.when(exists(up, right))(copies[k].start)

    def end(copies, ref, tiles, arrived, corner):
        for k, (up, right) in enumerate(AROUND):
            pl.when(exists(up, right))(copies[k].wait_send)
        for v in range(2):

            @pl.when(exists(2 * v - 1, 0))
            def _():
                copies[v].wait_recv()
                unpack(ref, tiles, v, arrived[v], first_col, cols)

        for k, (up, right) in enumerate(AROUND):
            if right != 0:
                pl.when(exists(-up, -right))(copies[k].wait_recv)
        for v in range(2):
            for h in range(2):

                @pl.when(exists(2 * v - 1, 2 * h - 1))
                def _():
                    unpack(ref, tiles, v, corner[v, h], SIDE if h == 0 else cols + first_col, SIDE)

    counts = jnp.zeros((n, 1), F32)
    for i in range(faces // CHUNK):
        here = slice(i * CHUNK, (i + 1) * CHUNK)
        owner_hot = one_hot(owner_ref[:, here].astype(F32), n)
        hot = owner_hot.astype(F32)
        running = jnp.dot(owner_hot, before, preferred_element_type=F32) + counts
        counts = counts + jnp.sum(hot, axis=1, keepdims=True)
        rank = jnp.sum(hot * running, axis=0, keepdims=True)
        rank_ref[:, here] = rank
        hots[:, here] = one_hot(rank, cap)
        parts = jnp.dot(gather, state_ref[:, here], preferred_element_type=F32)
        loads = (parts[:16] + parts[16:32] + parts[32:]) * scale_ref[:, here]
        element = element_ref[:, here]
        high_row = (element // cols).astype(F32)
        low_row = (element % cols).astype(F32)
        where_row = lax.broadcasted_iota(jnp.int32, loads.shape, 0)
        values = jnp.where(where_row == 12, high_row, jnp.where(where_row == 13, low_row, loads))
        high, low = split(values)
        highs[:, here] = high
        lows[:, here] = low
    pack(shell, 3, early)
    pl.semaphore_wait(barrier, n - 1)
    early_copies = neighbour_copies(shell, early, early_in, early_corner, 0)

    def value_copy(owner, slot):
        return pltpu.make_async_remote_copy(
            src_ref=outgoing.at[owner], dst_ref=incoming.at[slot], send_sem=send.at[owner],
            recv_sem=recv.at[slot], device_id=identity_of(owner, members), device_id_type=MESH)

    def number_copy(owner, slot):
        return pltpu.make_async_remote_copy(
            src_ref=number_out.at[owner], dst_ref=number_in.at[slot], send_sem=number_send.at[owner],
            recv_sem=number_recv.at[slot], device_id=identity_of(owner, members), device_id_type=MESH)

    blocks = n // BLOCK

    def send_block(t, carry):
        owners = [partner(me, turn_of(t * BLOCK + i, n, members, True), n) for i in range(BLOCK)]
        owner_wide = jnp.broadcast_to(owner_ref[...], (16, faces))
        high, low = highs[...], lows[...]
        pieces = []
        for i in range(BLOCK):
            here = owner_wide == owners[i]
            pieces.append(jnp.where(here, high, 0.0).astype(BF16))
            pieces.append(jnp.where(here, low, 0.0).astype(BF16))
        total = lax.dot_general(
            jnp.concatenate(pieces, axis=0), hots[...], NT, preferred_element_type=F32
        )
        for i in range(BLOCK):
            owner = owners[i]
            block = total[32 * i : 32 * i + 16] + total[32 * i + 16 : 32 * i + 32]
            number = (block[12:13] * cols + block[13:14]).astype(jnp.int32)
            lines = [block[:12, h * LANES : (h + 1) * LANES] for h in range(halves)]
            if deep > 12 * halves:
                lines.append(jnp.zeros((deep - 12 * halves, LANES), F32))
            block = jnp.concatenate(lines, axis=0)

            @pl.when(owner == me)
            def _():
                incoming[me] = block
                number_in[me] = number

            @pl.when(owner != me)
            def _():
                outgoing[owner] = block
                number_out[owner] = number
                number_copy(owner, me).start()
                value_copy(owner, me).start()
        return carry

    lax.fori_loop(0, blocks, send_block, 0)
    begin(early_copies, (True, False))
    total_load[...] = jnp.zeros_like(total_load)
    total_edge[...] = jnp.zeros_like(total_edge)
    total_inner[...] = jnp.zeros_like(total_inner)

    per = max(1, min(BLOCK, 1024 // cap))
    width = per * cap

    edge_rows, inner_rows = 12 * 2 * SWEEPS, 12 * (rows - 2 * SWEEPS)

    def level_rows(size, level):
        row = lax.broadcasted_iota(jnp.int32, (size, 1), 0) // 6
        return level(row) * layers

    edge_row = level_rows(2 * run, lambda i: jnp.where(i < halo, i, i + HIGH - 2 * halo))
    inner_row = level_rows(6 * HIGH - 2 * run, lambda i: i + halo)

    def take_sources(t, wait, with_edge, with_inner):
        sources = [partner(me, turn_of(t * per + i, n, members, COLLECT_FAR), n) for i in range(per)]
        if wait:
            for source in sources:

                @pl.when(source != me)
                def _():
                    number_copy(source, source).wait_recv()
                    value_copy(source, source).wait_recv()

        numbers, values = [], []
        for source in sources:
            numbers.append(number_in[source])
            value = incoming[source]
            for h in range(halves):
                values.append(value[12 * h : 12 * h + 12])
        number = jnp.concatenate(numbers, axis=1)
        value = jnp.concatenate(values, axis=1)
        row = number // cols
        low_hot = one_hot((number % cols).astype(F32), cols)
        lefts = []
        for part in split(value):
            tiles = [
                jnp.concatenate([part[component(t, 0) : component(t, 0) + 3],
                                 part[component(t, 3) : component(t, 3) + 3]] * 4, axis=0)
                for t in range(2)
            ]
            pieces = []
            for wanted, level in ((with_edge, edge_row), (with_inner, inner_row)):
                if wanted:
                    for k in range(layers):
                        mask = level + k == row
                        for t in range(2):
                            held = [tiles[t]] * (level.shape[0] // 24)
                            held = jnp.concatenate(held, axis=0) if len(held) > 1 else held[0]
                            pieces.append(jnp.where(mask, held, 0.0))
            lefts.append(jnp.concatenate(pieces, axis=0).astype(BF16))
        left = jnp.concatenate(lefts, axis=1)
        right = jnp.concatenate([low_hot, low_hot], axis=1)
        return lax.dot_general(left, right, NT, preferred_element_type=F32)

    def take_all(t, carry):
        total_load[...] += take_sources(t, True, True, True)
        return carry

    def take_edge(t, carry):
        total_edge[...] += take_sources(t, True, True, False)
        return carry

    def take_inner(t, carry):
        total_inner[...] += take_sources(t, False, False, True)
        return carry

    def placed(value, start, size, target):
        result = None
        for tile in range(start // LANES, (start + size - 1) // LANES + 1):
            end = min((tile + 1) * LANES, value.shape[1])
            piece = value[:, tile * LANES : end]
            if end < (tile + 1) * LANES:
                piece = jnp.concatenate([piece, jnp.zeros((cols, (tile + 1) * LANES - end), F32)], axis=1)
            turn = (target - start) % LANES
            piece = pltpu.roll(piece, turn, 1) if turn else piece
            first, last = max(start, tile * LANES), min(start + size, (tile + 1) * LANES)
            wanted = lanes_in(target + first - start, last - first)
            result = jnp.where(wanted, piece, 0.0 if result is None else result)
        return result

    steps = n // per
    split_at = steps - int(steps * SPLIT_PART)
    lax.fori_loop(0, split_at, take_all, 0)
    lax.fori_loop(split_at, steps, take_edge, 0)
    edge_total = (total_load[:edge_rows] + total_edge[...]).T
    for k in range(layers):
        inv = shell[k, inner, 2 * LANES :]
        for t in range(2):
            start = (2 * k + t) * 2 * run
            value = placed(edge_total, start, run, run) + placed(edge_total, start + run, run, 6 * HIGH)
            base[k, inner, t * LANES : (t + 1) * LANES] = value * inv
    pack(base, 2, late)
    late_copies = neighbour_copies(base, late, late_in, late_corner, 1)
    begin(late_copies, (False,))
    lax.fori_loop(split_at, steps, take_inner, 0)
    inner_total = (total_load[edge_rows:] + total_inner[...]).T
    for k in range(layers):
        inv = shell[k, inner, 2 * LANES :]
        for t in range(2):
            size = 6 * HIGH - 2 * run
            value = placed(inner_total, (2 * k + t) * size, size, 2 * run)
            there = slice(t * LANES, (t + 1) * LANES)
            base[k, inner, there] = base[k, inner, there] + value * inv
    begin(late_copies, (True,))
    end(early_copies, shell, 3, early_in, early_corner)
    end(late_copies, base, 2, late_in, late_corner)

    all_cols = cols + first_col
    here, east, west = (pl.ds(SIDE + move, all_cols) for move in (0, 1, -1))

    def relax(source, target):
        for k in range(layers):
            if k > 0:
                south = source[k - 1, here, LANES : 2 * LANES]
            else:
                south = pltpu.roll(source[layers - 1, here, LANES : 2 * LANES], 6, 1)
            if k < layers - 1:
                north = source[k + 1, here, :LANES]
            else:
                north = pltpu.roll(source[0, here, :LANES], LANES - 6, 1)
            first = jnp.where(first_half, source[k, east, :LANES], source[k, west, :LANES]) + south
            second = jnp.where(
                first_half, source[k, west, LANES : 2 * LANES], source[k, east, LANES : 2 * LANES]
            ) + north
            moved = times(jnp.concatenate([first, second], axis=1), couple_held[...])
            inv = shell[k, here, 2 * LANES :]
            target[k, here, : 2 * LANES] = base[k, here, :] + moved * jnp.concatenate([inv, inv], axis=1)

    def pair(_, carry):
        relax(shell, other)
        relax(other, shell)
        return carry

    lax.fori_loop(0, SWEEPS // 2, pair, 0)

    for k in range(layers):
        for t in range(2):
            for w in range(len(lane_tiles)):
                turned[k * 3 + t, w] = shell[k, first_col + w * LANES : first_col + (w + 1) * LANES,
                                             t * LANES : (t + 1) * LANES].T
                for q in range(6):
                    strides[w, component(t, q), pl.ds(k, HIGH, stride=layers), :] = (
                        turned[k * 3 + t, w, pl.ds(run + q, HIGH, stride=6), :])
    for w, tile in enumerate(lane_tiles):
        value = strides[w, :12]
        disp_held[:, :, tile] = value
        high, low = split(value.reshape(12 * rows, LANES))
        table[:, tile] = high.astype(BF16)
        table[:, cols + w * LANES : cols + (w + 1) * LANES] = low.astype(BF16)
    disp_copy = pltpu.make_async_copy(disp_held, disp_ref, disp_sem)
    disp_copy.start()

    spread = exact(
        pick((8 * NODES_F, NODES_F), lambda i: i // 8, lambda j: j),
        exact(transfer_ref[...], pick((4, 12), lambda i: i, lambda j: j // 3), (((0,), (0,)), ((), ()))),
    )
    spread = jnp.where(same(spread.shape, lambda i: i % 8, lambda j: j % 3), spread, 0.0)

    def back_copy(owner, slot):
        return pltpu.make_async_remote_copy(
            src_ref=answers.at[owner], dst_ref=answered.at[slot], send_sem=back_send.at[owner],
            recv_sem=back_recv.at[slot], device_id=identity_of(owner, members), device_id_type=MESH)

    def answer(t, carry):
        sources = [partner(me, turn_of(t * per + i, n, members, True), n) for i in range(per)]
        number = jnp.concatenate([number_in[source] for source in sources], axis=1)
        mask = lax.broadcasted_iota(jnp.int32, (rows, width), 0) == number // cols
        low_hot = one_hot((number % cols).astype(F32), cols)
        picked = jnp.dot(
            table[...], jnp.concatenate([low_hot, low_hot], axis=0), preferred_element_type=F32
        )
        lines = [
            jnp.sum(jnp.where(mask, picked[c * rows : (c + 1) * rows], 0.0), axis=0, keepdims=True)
            for c in range(12)
        ]
        result = jnp.concatenate(lines, axis=0)
        for i, source in enumerate(sources):
            parts = [
                result[:, i * cap + h * LANES : i * cap + (h + 1) * LANES] for h in range(halves)
            ]
            if deep > 12 * halves:
                parts.append(jnp.zeros((deep - 12 * halves, LANES), F32))
            block = jnp.concatenate(parts, axis=0)

            @pl.when(source == me)
            def _():
                answered[me] = block

            @pl.when(source != me)
            def _():
                answers[source] = block
                back_copy(source, me).start()
        return carry

    lax.fori_loop(0, n // per, answer, 0)

    def prepare(i, carry):
        here = pl.ds(pl.multiple_of(i * CHUNK, CHUNK), CHUNK)
        rank = rank_ref[:, here].astype(jnp.int32)
        hot = one_hot((rank % LANES).astype(F32), LANES)
        lane_hots[:, here] = jnp.concatenate([hot, hot], axis=0)
        return carry

    lax.fori_loop(0, faces // CHUNK, prepare, 0)

    def take_block(t, carry):
        sources = [partner(me, turn_of(t * BLOCK + i, n, members, TAKE_FAR), n) for i in range(BLOCK)]
        lines = []
        for source in sources:

            @pl.when(source != me)
            def _():
                back_copy(source, source).wait_recv()

            lines.append(answered[source])
        high, low = split(jnp.concatenate(lines, axis=0))
        held = jnp.concatenate([high.astype(BF16), low.astype(BF16)], axis=1)

        for j in range(faces // CHUNK):
            here = slice(j * CHUNK, (j + 1) * CHUNK)
            picked = jnp.dot(held, lane_hots[:, here], preferred_element_type=F32)
            owner = jnp.broadcast_to(owner_ref[:, here], (deep, CHUNK))
            value = found[:, here]
            for i in range(BLOCK):
                value = jnp.where(owner == sources[i], picked[i * deep : (i + 1) * deep], value)
            found[:, here] = value
        return carry

    found[...] = jnp.zeros_like(found)
    lax.fori_loop(0, blocks, take_block, 0)

    high = spread.astype(BF16)
    low = (spread - high.astype(F32)).astype(BF16)
    held = jnp.concatenate([high, high, low], axis=1)
    for j in range(faces // CHUNK):
        here = slice(j * CHUNK, (j + 1) * CHUNK)
        part = rank_ref[:, here].astype(jnp.int32) // LANES
        node = found[:12, here]
        for h in range(1, halves):
            node = jnp.where(part == h, found[12 * h : 12 * h + 12, here], node)
        high = node.astype(BF16)
        low = (node - high.astype(F32)).astype(BF16)
        faced = jnp.dot(
            held, jnp.concatenate([high, low, high], axis=0), preferred_element_type=F32
        )
        for k in range(NODES_F):
            out_ref[k, :, here] = faced[8 * k : 8 * k + 3]

    disp_copy.wait()

    def finish(k, carry):
        owner = lax.rem(me + k, n)
        number_copy(owner, me).wait_send()
        value_copy(owner, me).wait_send()
        back_copy(owner, me).wait_send()
        return carry

    lax.fori_loop(1, n, finish, 0)


def outward(cap, owner, element, state, lift, scale, transfer, stiffness, prev, factor):
    groups, members = lax.axis_size("grp"), lax.axis_size("dev")
    n = groups * members
    faces = owner.shape[1]
    _, rows, cols = prev.shape
    halves, deep = place_of(cap)
    layers = rows // HIGH
    tall = cols + 4 * SIDE
    near = [pltpu.VMEM((2, cols, LANES), F32), pltpu.VMEM((2, cols, LANES), F32),
            pltpu.VMEM((2, 2, SIDE, LANES), F32)]
    return pl.pallas_call(
        functools.partial(step_kernel, n, groups, members, cap, rows, cols),
        in_specs=[VM] * 9,
        out_specs=[ANY, VM],
        out_shape=[jax.ShapeDtypeStruct((12, rows, cols), F32),
                   jax.ShapeDtypeStruct((NODES_F, 3, faces), F32)],
        scratch_shapes=[
            pltpu.VMEM((16, faces), F32), pltpu.VMEM((16, faces), F32), pltpu.VMEM((cap, faces), BF16),
            pltpu.VMEM((n, deep, LANES), F32), pltpu.VMEM((n, deep, LANES), F32),
            pltpu.VMEM((n, 1, cap), jnp.int32), pltpu.VMEM((n, 1, cap), jnp.int32),
            pltpu.VMEM((1, faces), F32),
            pltpu.VMEM((layers, tall, 3 * LANES), F32), pltpu.VMEM((layers, tall, 2 * LANES), F32),
            pltpu.VMEM((layers, tall, 2 * LANES), F32), pltpu.VMEM((3 * layers, cols // LANES, LANES, LANES), F32),
            pltpu.VMEM((cols // LANES, 13, rows, LANES), F32), pltpu.VMEM((12 * rows, cols), F32),
            pltpu.VMEM((24 * SWEEPS, cols), F32), pltpu.VMEM((12 * rows - 24 * SWEEPS, cols), F32),
            pltpu.VMEM((6 * LANES, 2 * LANES), BF16),
        ] + near + near + [
            pltpu.VMEM((12 * rows, 2 * cols), BF16), pltpu.VMEM((2 * LANES, faces), BF16),
            pltpu.VMEM((deep, faces), F32),
            pltpu.VMEM((n, deep, LANES), F32), pltpu.VMEM((n, deep, LANES), F32),
        ] + [pltpu.SemaphoreType.DMA((n,))] * 4 + [pltpu.SemaphoreType.DMA((2, 8))] * 2
        + [pltpu.SemaphoreType.DMA((n,))] * 2
        + [pltpu.VMEM((12, rows, cols), F32), pltpu.SemaphoreType.DMA],
        compiler_params=pltpu.CompilerParams(
            collective_id=1, has_side_effects=True, vmem_limit_bytes=VMEM_LIMIT),
        name="step",
    )(owner, element, state, lift, scale, transfer, stiffness, prev, factor)


def deliver_kernel(disp_ref, face_ref, disp_out, face_out):
    disp_out[...] = disp_ref[...]
    face_out[...] = face_ref[...]


def deliver(disp, face):
    cut = 2
    specs = [pl.BlockSpec((a.shape[0] // cut,) + a.shape[1:], lambda i: (i, 0, 0)) for a in (disp, face)]
    return pl.pallas_call(
        deliver_kernel,
        grid=(cut,),
        in_specs=specs,
        out_specs=specs,
        out_shape=[jax.ShapeDtypeStruct(a.shape, F32) for a in (disp, face)],
        name="deliver",
    )(disp, face)


def local(
    face_owner,
    face_element,
    element_state,
    lift,
    face_scale,
    transfer,
    stiffness_ref,
    element_scale,
    displacement_prev,
):
    n = lax.axis_size("grp") * lax.axis_size("dev")
    faces = face_owner.shape[0]
    cap = -(-(2 * faces // n) // LANES) * LANES
    rows, cols = element_scale.shape
    prev = displacement_prev.reshape(12, rows, cols)
    owner = face_owner.reshape(1, faces)
    disp, face_displacement = outward(
        cap, owner, face_element.reshape(1, faces), element_state, lift,
        face_scale.reshape(1, faces), transfer, stiffness_ref, prev, element_scale,
    )
    disp, face_displacement = deliver(disp, face_displacement)
    return (disp.reshape(4, 3, rows, cols), face_displacement.transpose(1, 0, 2))


def solution(mesh):
    placed = (
        P(("grp", "dev"), None),
        P(("grp", "dev")),
        P(None, ("grp", "dev")),
        P(),
        P(("grp", "dev")),
        P(),
        P(),
        P("grp", "dev"),
        P(None, None, "grp", "dev"),
    )
    return jax.shard_map(
        local,
        mesh=mesh,
        in_specs=placed,
        out_specs=(P(None, None, "grp", "dev"), P(None, None, ("grp", "dev"))),
        check_vma=False,
    )
```

```python
import functools

import jax
import jax.numpy as jnp
from jax import lax
from jax.experimental import pallas as pl
from jax.experimental.pallas import tpu as pltpu
from jax.sharding import PartitionSpec as P

NODES_F = 10
SWEEPS = 8
LANES = 128
VMEM_LIMIT = 56 * 1024 * 1024

coupling_weight = 2.2
highest = lax.Precision.HIGHEST
F32 = jnp.float32
BF16 = jnp.bfloat16
NT = (((1,), (1,)), ((), ()))
VM = pl.BlockSpec(memory_space=pltpu.VMEM)
SM = pl.BlockSpec(memory_space=pltpu.SMEM)


def split(x):
    high = x.astype(BF16).astype(F32)
    return high, x - high


def one_hot(row, count):
    places = lax.broadcasted_iota(jnp.int32, (count, row.shape[1]), 0).astype(F32)
    return jnp.where(places == row, 1.0, 0.0).astype(BF16)


MESH = pl.DeviceIdType.MESH
ANY = pl.BlockSpec(memory_space=pl.ANY)
BLOCK = 8
COLLECT_FAR = False
SPLIT_PART = 0.75
TAKE_FAR = True
CHUNK = 512


def triple(x):
    high = x.astype(BF16)
    rest = x - high.astype(F32)
    middle = rest.astype(BF16)
    return high, middle, (rest - middle.astype(F32)).astype(BF16)


def exact(a, b, dims=(((1,), (0,)), ((), ()))):
    return lax.dot_general(a, b, dims, precision=highest, preferred_element_type=F32)


def same(shape, of_row, of_col):
    left = of_row(lax.broadcasted_iota(jnp.int32, (shape[0], 1), 0))
    return left == of_col(lax.broadcasted_iota(jnp.int32, (1, shape[1]), 1))


def pick(shape, of_row, of_col):
    return jnp.where(same(shape, of_row, of_col), 1.0, 0.0).astype(F32)


def place_of(cap):
    halves = cap // LANES
    return halves, -(-12 * halves // 8) * 8


def identity_of(t, members):
    return (t // members, lax.rem(t, members))


def partner(me, k, n):
    other, bit = 0, 1
    while bit < n:
        a, b = lax.rem(lax.div(me, bit), 2), lax.rem(lax.div(k, bit), 2)
        other = other + bit * (a + b - 2 * a * b)
        bit *= 2
    return other


def turn_of(m, n, members, far_first):
    half, near = n // 2, members // 2
    part, m = lax.div(m, half), lax.rem(m, half)
    top = 1 - part if far_first else part
    row, rows_of = lax.div(m, near) * 2, n // members
    row = lax.rem(row, rows_of) + lax.div(row, rows_of)
    return row * members + top * near + lax.rem(m, near)


def greet_all(n, members, me):
    barrier = pltpu.get_barrier_semaphore()

    def greet(k, carry):
        pl.semaphore_signal(
            barrier, inc=1, device_id=identity_of(lax.rem(me + k, n), members), device_id_type=MESH
        )
        return carry

    lax.fori_loop(1, n, greet, 0)
    return barrier


AROUND = [(1, 0), (-1, 0), (0, 1), (0, -1), (1, 1), (1, -1), (-1, 1), (-1, -1)]
HIGH = 16
SIDE = 8


def node_of(t, q):
    return jnp.where(t == 0, q // 3, 3 - q // 3)


def mixing(inverse, levels):
    def lanes_at(shape, axis):
        lane = lax.broadcasted_iota(jnp.int32, shape, axis)
        t, l = lane // LANES, lane % LANES
        return t, l % 6, jnp.where(l < 6 * levels, l // 6, -1 - axis)

    def ones(condition):
        return jnp.where(condition, 1.0, 0.0).astype(F32)

    wide = 2 * LANES
    t, q, target_level = lanes_at((1, wide), 1)
    to = ones(lax.broadcasted_iota(jnp.int32, (12, wide), 0) == 3 * node_of(t, q) + q % 3)
    t, q, level = lanes_at((wide, 1), 0)
    source = 3 * jnp.where(t == 0, 1 - q // 3, 2 + q // 3) + q % 3
    out = ones(lax.broadcasted_iota(jnp.int32, (wide, 12), 1) == source)
    couple = exact(exact(out, inverse, NT), to) * coupling_weight
    return jnp.where(level == target_level, couple, 0.0)


def stacked(matrix):
    high = matrix.astype(BF16)
    low = (matrix - high.astype(F32)).astype(BF16)
    return jnp.concatenate([high, high, low], axis=0)


def times(x, held):
    high = x.astype(BF16)
    low = (x - high.astype(F32)).astype(BF16)
    return jnp.dot(jnp.concatenate([high, low, high], axis=1), held, preferred_element_type=F32)


def step_kernel(n, groups, members, cap, rows, cols, owner_ref, element_ref, state_ref, lift_ref,
                   scale_ref, transfer_ref, stiff_ref, prev_ref, factor_ref,
                   disp_ref, out_ref,
                   highs, lows, hots, outgoing, incoming, number_out, number_in, rank_ref,
                   shell, other, base, turned, strides, total_load, total_edge, total_inner,
                   couple_held, early, early_in, early_corner, late, late_in, late_corner,
                   table, lane_hots, found, answers, answered,
                   send, recv, number_send, number_recv, near_send, near_recv, back_send, back_recv, disp_held, disp_sem):
    g, d = lax.axis_index("grp"), lax.axis_index("dev")
    me = g * members + d
    faces = owner_ref.shape[1]
    halves, deep = place_of(cap)
    layers = rows // HIGH
    halo = SWEEPS // layers
    levels = HIGH + 2 * halo
    run = 6 * halo
    first_col = 2 * SIDE
    inner = slice(first_col, first_col + cols)

    shell[...] = jnp.zeros_like(shell)
    base[...] = jnp.zeros_like(base)
    turned[...] = jnp.zeros_like(turned)
    barrier = greet_all(n, members, me)

    def component(t, q):
        return 3 * (q // 3 if t == 0 else 3 - q // 3) + q % 3

    lane_tiles = [slice(w * LANES, (w + 1) * LANES) for w in range(cols // LANES)]
    for w, tile in enumerate(lane_tiles):
        strides[w, :12] = prev_ref[:, :, tile]
        strides[w, 12] = 1.0 / factor_ref[:, tile]
    for k in range(layers):
        for t in range(3):
            for w in range(len(lane_tiles)):
                for q in range(6):
                    turned[k * 3 + t, w, pl.ds(run + q, HIGH, stride=6), :] = (
                        strides[w, component(t, q) if t < 2 else 12, pl.ds(k, HIGH, stride=layers), :])
                shell[k, first_col + w * LANES : first_col + (w + 1) * LANES,
                      t * LANES : (t + 1) * LANES] = turned[k * 3 + t, w].T

    stiffness = stiff_ref[...]
    identity = pick((12, 12), lambda i: i, lambda j: j)
    approx = identity / 5.0
    rest = identity - stiffness / 5.0
    for _ in range(8):
        both = exact(jnp.concatenate([approx, rest], axis=0), rest)
        approx, rest = approx + both[:12], both[12:]

    spread = exact(exact(pick((16, 4), lambda i: i // 3, lambda j: j), transfer_ref[...]),
                   pick((NODES_F, 3 * NODES_F), lambda i: i, lambda j: j % NODES_F))
    kept = same(spread.shape, lambda i: i % 3, lambda j: j // NODES_F)
    kept = kept & (lax.broadcasted_iota(jnp.int32, spread.shape, 0) < 12)
    spread = jnp.where(kept, spread, 0.0)[:12]
    spread = jnp.concatenate([exact(approx, spread), jnp.zeros((4, spread.shape[1]), F32)], axis=0)
    gather = jnp.concatenate(triple(exact(spread, lift_ref[...].astype(F32))), axis=0)
    before = jnp.where(
        lax.broadcasted_iota(jnp.int32, (CHUNK, CHUNK), 0)
        < lax.broadcasted_iota(jnp.int32, (CHUNK, CHUNK), 1), 1.0, 0.0
    ).astype(BF16)

    lane = lax.broadcasted_iota(jnp.int32, (1, LANES), 1)

    def lanes_in(start, size):
        return (lane >= start) & (lane < start + size)

    first_half = lax.rem(lane, 6) < 3

    def slot_of(k, t):
        return run * (2 * k + t if t < 2 else 2 * layers + k // 2)

    def pack(ref, tiles, target):
        for v in range(2):
            start = run if v == 1 else 6 * HIGH
            packed = jnp.zeros((cols, LANES), F32)
            for k in range(layers):
                for t in range(tiles):
                    move = slot_of(k, t)
                    turn = (move - start) % LANES
                    piece = ref[k, inner, t * LANES : (t + 1) * LANES]
                    piece = pltpu.roll(piece, turn, 1) if turn else piece
                    wanted = lanes_in(move, run)
                    if t == 2:
                        wanted = wanted & (first_half == (k % 2 == 0))
                    packed = jnp.where(wanted, piece, packed)
            target[v] = packed

    def unpack(ref, tiles, v, arrived, start, size):
        goal = 0 if v == 0 else run + 6 * HIGH
        keep = lanes_in(goal, run)
        for k in range(layers):
            for t in range(tiles):
                turn = (goal - slot_of(k, t)) % LANES
                piece = pltpu.roll(arrived, turn, 1) if turn else arrived
                if t == 2:
                    piece = jnp.where(first_half == (k % 2 == 0), piece,
                                      pltpu.roll(piece, 3 if k % 2 == 0 else LANES - 3, 1))
                here = slice(start, start + size)
                there = slice(t * LANES, (t + 1) * LANES)
                ref[k, here, there] = jnp.where(keep, piece, ref[k, here, there])

    def exists(up, right):
        row, col = g + up, d + right
        return (row >= 0) & (row < groups) & (col >= 0) & (col < members)

    def neighbour_copies(ref, packed, arrived, corner, number):
        copies = []
        for k, (up, right) in enumerate(AROUND):
            v, h = (0 if up == 1 else 1), (0 if right == 1 else 1)
            if right == 0:
                source, target = packed.at[v], arrived.at[v]
            elif up == 0:
                start, end = (cols + SIDE, SIDE) if right == 1 else (first_col, cols + first_col)
                source, target = ref.at[:, pl.ds(start, SIDE), :], ref.at[:, pl.ds(end, SIDE), :]
            else:
                start = cols - SIDE if right == 1 else 0
                source, target = packed.at[v, pl.ds(start, SIDE), :], corner.at[v, h]
            copies.append(pltpu.make_async_remote_copy(
                src_ref=source, dst_ref=target, send_sem=near_send.at[number, k],
                recv_sem=near_recv.at[number, k],
                device_id=(g + up, d + right), device_id_type=MESH))
        return copies

    def begin(copies, kinds):
        for k, (up, right) in enumerate(AROUND):
            if (up == 0) in kinds:
                pl.when(exists(up, right))(copies[k].start)

    def end(copies, ref, tiles, arrived, corner):
        for k, (up, right) in enumerate(AROUND):
            pl.when(exists(up, right))(copies[k].wait_send)
        for v in range(2):

            @pl.when(exists(2 * v - 1, 0))
            def _():
                copies[v].wait_recv()
                unpack(ref, tiles, v, arrived[v], first_col, cols)

        for k, (up, right) in enumerate(AROUND):
            if right != 0:
                pl.when(exists(-up, -right))(copies[k].wait_recv)
        for v in range(2):
            for h in range(2):

                @pl.when(exists(2 * v - 1, 2 * h - 1))
                def _():
                    unpack(ref, tiles, v, corner[v, h], SIDE if h == 0 else cols + first_col, SIDE)

    counts = jnp.zeros((n, 1), F32)
    for i in range(faces // CHUNK):
        here = slice(i * CHUNK, (i + 1) * CHUNK)
        owner_hot = one_hot(owner_ref[:, here].astype(F32), n)
        hot = owner_hot.astype(F32)
        running = jnp.dot(owner_hot, before, preferred_element_type=F32) + counts
        counts = counts + jnp.sum(hot, axis=1, keepdims=True)
        rank = jnp.sum(hot * running, axis=0, keepdims=True)
        rank_ref[:, here] = rank
        hots[:, here] = one_hot(rank, cap)
        parts = jnp.dot(gather, state_ref[:, here], preferred_element_type=F32)
        loads = (parts[:16] + parts[16:32] + parts[32:]) * scale_ref[:, here]
        element = element_ref[:, here]
        high_row = (element // cols).astype(F32)
        low_row = (element % cols).astype(F32)
        where_row = lax.broadcasted_iota(jnp.int32, loads.shape, 0)
        values = jnp.where(where_row == 12, high_row, jnp.where(where_row == 13, low_row, loads))
        high, low = split(values)
        highs[:, here] = high
        lows[:, here] = low
    pack(shell, 3, early)
    pl.semaphore_wait(barrier, n - 1)
    early_copies = neighbour_copies(shell, early, early_in, early_corner, 0)

    def value_copy(owner, slot):
        return pltpu.make_async_remote_copy(
            src_ref=outgoing.at[owner], dst_ref=incoming.at[slot], send_sem=send.at[owner],
            recv_sem=recv.at[slot], device_id=identity_of(owner, members), device_id_type=MESH)

    def number_copy(owner, slot):
        return pltpu.make_async_remote_copy(
            src_ref=number_out.at[owner], dst_ref=number_in.at[slot], send_sem=number_send.at[owner],
            recv_sem=number_recv.at[slot], device_id=identity_of(owner, members), device_id_type=MESH)

    blocks = n // BLOCK

    def send_block(t, carry):
        owners = [partner(me, turn_of(t * BLOCK + i, n, members, True), n) for i in range(BLOCK)]
        owner_wide = jnp.broadcast_to(owner_ref[...], (16, faces))
        high, low = highs[...], lows[...]
        pieces = []
        for i in range(BLOCK):
            here = owner_wide == owners[i]
            pieces.append(jnp.where(here, high, 0.0).astype(BF16))
            pieces.append(jnp.where(here, low, 0.0).astype(BF16))
        total = lax.dot_general(
            jnp.concatenate(pieces, axis=0), hots[...], NT, preferred_element_type=F32
        )
        for i in range(BLOCK):
            owner = owners[i]
            block = total[32 * i : 32 * i + 16] + total[32 * i + 16 : 32 * i + 32]
            number = (block[12:13] * cols + block[13:14]).astype(jnp.int32)
            lines = [block[:12, h * LANES : (h + 1) * LANES] for h in range(halves)]
            if deep > 12 * halves:
                lines.append(jnp.zeros((deep - 12 * halves, LANES), F32))
            block = jnp.concatenate(lines, axis=0)

            @pl.when(owner == me)
            def _():
                incoming[me] = block
                number_in[me] = number

            @pl.when(owner != me)
            def _():
                outgoing[owner] = block
                number_out[owner] = number
                number_copy(owner, me).start()
                value_copy(owner, me).start()
        return carry

    lax.fori_loop(0, blocks, send_block, 0)
    begin(early_copies, (True, False))
    other[...] = jnp.zeros_like(other)
    couple_held[...] = stacked(mixing(approx, levels))

    def prepare(i, carry):
        here = pl.ds(pl.multiple_of(i * CHUNK, CHUNK), CHUNK)
        rank = rank_ref[:, here].astype(jnp.int32)
        hot = one_hot((rank % LANES).astype(F32), LANES)
        lane_hots[:, here] = jnp.concatenate([hot, hot], axis=0)
        return carry

    lax.fori_loop(0, faces // CHUNK, prepare, 0)

    total_load[...] = jnp.zeros_like(total_load)
    total_edge[...] = jnp.zeros_like(total_edge)
    total_inner[...] = jnp.zeros_like(total_inner)

    per = max(1, min(BLOCK, 1024 // cap))
    width = per * cap

    edge_rows, inner_rows = 12 * 2 * SWEEPS, 12 * (rows - 2 * SWEEPS)

    def level_rows(size, level):
        row = lax.broadcasted_iota(jnp.int32, (size, 1), 0) // 6
        return level(row) * layers

    edge_row = level_rows(2 * run, lambda i: jnp.where(i < halo, i, i + HIGH - 2 * halo))
    inner_row = level_rows(6 * HIGH - 2 * run, lambda i: i + halo)

    def take_sources(t, wait, with_edge, with_inner):
        sources = [partner(me, turn_of(t * per + i, n, members, COLLECT_FAR), n) for i in range(per)]
        if wait:
            for source in sources:

                @pl.when(source != me)
                def _():
                    number_copy(source, source).wait_recv()
                    value_copy(source, source).wait_recv()

        numbers, values = [], []
        for source in sources:
            numbers.append(number_in[source])
            value = incoming[source]
            for h in range(halves):
                values.append(value[12 * h : 12 * h + 12])
        number = jnp.concatenate(numbers, axis=1)
        value = jnp.concatenate(values, axis=1)
        row = number // cols
        low_hot = one_hot((number % cols).astype(F32), cols)
        lefts = []
        for part in split(value):
            tiles = [
                jnp.concatenate([part[component(t, 0) : component(t, 0) + 3],
                                 part[component(t, 3) : component(t, 3) + 3]] * 4, axis=0)
                for t in range(2)
            ]
            pieces = []
            for wanted, level in ((with_edge, edge_row), (with_inner, inner_row)):
                if wanted:
                    for k in range(layers):
                        mask = level + k == row
                        for t in range(2):
                            held = [tiles[t]] * (level.shape[0] // 24)
                            held = jnp.concatenate(held, axis=0) if len(held) > 1 else held[0]
                            pieces.append(jnp.where(mask, held, 0.0))
            lefts.append(jnp.concatenate(pieces, axis=0).astype(BF16))
        left = jnp.concatenate(lefts, axis=1)
        right = jnp.concatenate([low_hot, low_hot], axis=1)
        return lax.dot_general(left, right, NT, preferred_element_type=F32)

    def take_all(t, carry):
        total_load[...] += take_sources(t, True, True, True)
        return carry

    def take_edge(t, carry):
        total_edge[...] += take_sources(t, True, True, False)
        return carry

    def take_inner(t, carry):
        total_inner[...] += take_sources(t, False, False, True)
        return carry

    def placed(value, start, size, target):
        result = None
        for tile in range(start // LANES, (start + size - 1) // LANES + 1):
            end = min((tile + 1) * LANES, value.shape[1])
            piece = value[:, tile * LANES : end]
            if end < (tile + 1) * LANES:
                piece = jnp.concatenate([piece, jnp.zeros((cols, (tile + 1) * LANES - end), F32)], axis=1)
            turn = (target - start) % LANES
            piece = pltpu.roll(piece, turn, 1) if turn else piece
            first, last = max(start, tile * LANES), min(start + size, (tile + 1) * LANES)
            wanted = lanes_in(target + first - start, last - first)
            result = jnp.where(wanted, piece, 0.0 if result is None else result)
        return result

    steps = n // per
    split_at = steps - int(steps * SPLIT_PART)
    lax.fori_loop(0, split_at, take_all, 0)
    lax.fori_loop(split_at, steps, take_edge, 0)
    edge_total = (total_load[:edge_rows] + total_edge[...]).T
    for k in range(layers):
        inv = shell[k, inner, 2 * LANES :]
        for t in range(2):
            start = (2 * k + t) * 2 * run
            value = placed(edge_total, start, run, run) + placed(edge_total, start + run, run, 6 * HIGH)
            base[k, inner, t * LANES : (t + 1) * LANES] = value * inv
    pack(base, 2, late)
    late_copies = neighbour_copies(base, late, late_in, late_corner, 1)
    begin(late_copies, (False,))
    lax.fori_loop(split_at, steps, take_inner, 0)
    inner_total = (total_load[edge_rows:] + total_inner[...]).T
    for k in range(layers):
        inv = shell[k, inner, 2 * LANES :]
        for t in range(2):
            size = 6 * HIGH - 2 * run
            value = placed(inner_total, (2 * k + t) * size, size, 2 * run)
            there = slice(t * LANES, (t + 1) * LANES)
            base[k, inner, there] = base[k, inner, there] + value * inv
    begin(late_copies, (True,))
    end(early_copies, shell, 3, early_in, early_corner)
    end(late_copies, base, 2, late_in, late_corner)

    all_cols = cols + first_col
    here, east, west = (pl.ds(SIDE + move, all_cols) for move in (0, 1, -1))

    def relax(source, target):
        for k in range(layers):
            if k > 0:
                south = source[k - 1, here, LANES : 2 * LANES]
            else:
                south = pltpu.roll(source[layers - 1, here, LANES : 2 * LANES], 6, 1)
            if k < layers - 1:
                north = source[k + 1, here, :LANES]
            else:
                north = pltpu.roll(source[0, here, :LANES], LANES - 6, 1)
            first = jnp.where(first_half, source[k, east, :LANES], source[k, west, :LANES]) + south
            second = jnp.where(
                first_half, source[k, west, LANES : 2 * LANES], source[k, east, LANES : 2 * LANES]
            ) + north
            moved = times(jnp.concatenate([first, second], axis=1), couple_held[...])
            inv = shell[k, here, 2 * LANES :]
            target[k, here, : 2 * LANES] = base[k, here, :] + moved * jnp.concatenate([inv, inv], axis=1)

    def pair(_, carry):
        relax(shell, other)
        relax(other, shell)
        return carry

    lax.fori_loop(0, SWEEPS // 2, pair, 0)

    for k in range(layers):
        for t in range(2):
            for w in range(len(lane_tiles)):
                turned[k * 3 + t, w] = shell[k, first_col + w * LANES : first_col + (w + 1) * LANES,
                                             t * LANES : (t + 1) * LANES].T
                for q in range(6):
                    strides[w, component(t, q), pl.ds(k, HIGH, stride=layers), :] = (
                        turned[k * 3 + t, w, pl.ds(run + q, HIGH, stride=6), :])
    for w, tile in enumerate(lane_tiles):
        value = strides[w, :12]
        disp_held[:, :, tile] = value
        high, low = split(value.reshape(12 * rows, LANES))
        table[:, tile] = high.astype(BF16)
        table[:, cols + w * LANES : cols + (w + 1) * LANES] = low.astype(BF16)
    disp_copy = pltpu.make_async_copy(disp_held, disp_ref, disp_sem)
    disp_copy.start()

    spread = exact(
        pick((8 * NODES_F, NODES_F), lambda i: i // 8, lambda j: j),
        exact(transfer_ref[...], pick((4, 12), lambda i: i, lambda j: j // 3), (((0,), (0,)), ((), ()))),
    )
    spread = jnp.where(same(spread.shape, lambda i: i % 8, lambda j: j % 3), spread, 0.0)

    def back_copy(owner, slot):
        return pltpu.make_async_remote_copy(
            src_ref=answers.at[owner], dst_ref=answered.at[slot], send_sem=back_send.at[owner],
            recv_sem=back_recv.at[slot], device_id=identity_of(owner, members), device_id_type=MESH)

    def answer(t, carry):
        sources = [partner(me, turn_of(t * per + i, n, members, True), n) for i in range(per)]
        number = jnp.concatenate([number_in[source] for source in sources], axis=1)
        mask = lax.broadcasted_iota(jnp.int32, (rows, width), 0) == number // cols
        low_hot = one_hot((number % cols).astype(F32), cols)
        picked = jnp.dot(
            table[...], jnp.concatenate([low_hot, low_hot], axis=0), preferred_element_type=F32
        )
        lines = [
            jnp.sum(jnp.where(mask, picked[c * rows : (c + 1) * rows], 0.0), axis=0, keepdims=True)
            for c in range(12)
        ]
        result = jnp.concatenate(lines, axis=0)
        for i, source in enumerate(sources):
            parts = [
                result[:, i * cap + h * LANES : i * cap + (h + 1) * LANES] for h in range(halves)
            ]
            if deep > 12 * halves:
                parts.append(jnp.zeros((deep - 12 * halves, LANES), F32))
            block = jnp.concatenate(parts, axis=0)

            @pl.when(source == me)
            def _():
                answered[me] = block

            @pl.when(source != me)
            def _():
                answers[source] = block
                back_copy(source, me).start()
        return carry

    lax.fori_loop(0, n // per, answer, 0)

    def take_block(t, carry):
        sources = [partner(me, turn_of(t * BLOCK + i, n, members, TAKE_FAR), n) for i in range(BLOCK)]
        lines = []
        for source in sources:

            @pl.when(source != me)
            def _():
                back_copy(source, source).wait_recv()

            lines.append(answered[source])
        high, low = split(jnp.concatenate(lines, axis=0))
        held = jnp.concatenate([high.astype(BF16), low.astype(BF16)], axis=1)

        for j in range(faces // CHUNK):
            here = slice(j * CHUNK, (j + 1) * CHUNK)
            picked = jnp.dot(held, lane_hots[:, here], preferred_element_type=F32)
            owner = jnp.broadcast_to(owner_ref[:, here], (deep, CHUNK))
            value = found[:, here]
            for i in range(BLOCK):
                value = jnp.where(owner == sources[i], picked[i * deep : (i + 1) * deep], value)
            found[:, here] = value
        return carry

    found[...] = jnp.zeros_like(found)
    lax.fori_loop(0, blocks, take_block, 0)

    high = spread.astype(BF16)
    low = (spread - high.astype(F32)).astype(BF16)
    held = jnp.concatenate([high, high, low], axis=1)
    for j in range(faces // CHUNK):
        here = slice(j * CHUNK, (j + 1) * CHUNK)
        part = rank_ref[:, here].astype(jnp.int32) // LANES
        node = found[:12, here]
        for h in range(1, halves):
            node = jnp.where(part == h, found[12 * h : 12 * h + 12, here], node)
        high = node.astype(BF16)
        low = (node - high.astype(F32)).astype(BF16)
        faced = jnp.dot(
            held, jnp.concatenate([high, low, high], axis=0), preferred_element_type=F32
        )
        for k in range(NODES_F):
            out_ref[k, :, here] = faced[8 * k : 8 * k + 3]

    disp_copy.wait()

    def finish(k, carry):
        owner = lax.rem(me + k, n)
        number_copy(owner, me).wait_send()
        value_copy(owner, me).wait_send()
        back_copy(owner, me).wait_send()
        return carry

    lax.fori_loop(1, n, finish, 0)


def outward(cap, owner, element, state, lift, scale, transfer, stiffness, prev, factor):
    groups, members = lax.axis_size("grp"), lax.axis_size("dev")
    n = groups * members
    faces = owner.shape[1]
    _, rows, cols = prev.shape
    halves, deep = place_of(cap)
    layers = rows // HIGH
    tall = cols + 4 * SIDE
    near = [pltpu.VMEM((2, cols, LANES), F32), pltpu.VMEM((2, cols, LANES), F32),
            pltpu.VMEM((2, 2, SIDE, LANES), F32)]
    return pl.pallas_call(
        functools.partial(step_kernel, n, groups, members, cap, rows, cols),
        in_specs=[VM] * 9,
        out_specs=[ANY, VM],
        out_shape=[jax.ShapeDtypeStruct((12, rows, cols), F32),
                   jax.ShapeDtypeStruct((NODES_F, 3, faces), F32)],
        scratch_shapes=[
            pltpu.VMEM((16, faces), F32), pltpu.VMEM((16, faces), F32), pltpu.VMEM((cap, faces), BF16),
            pltpu.VMEM((n, deep, LANES), F32), pltpu.VMEM((n, deep, LANES), F32),
            pltpu.VMEM((n, 1, cap), jnp.int32), pltpu.VMEM((n, 1, cap), jnp.int32),
            pltpu.VMEM((1, faces), F32),
            pltpu.VMEM((layers, tall, 3 * LANES), F32), pltpu.VMEM((layers, tall, 2 * LANES), F32),
            pltpu.VMEM((layers, tall, 2 * LANES), F32), pltpu.VMEM((3 * layers, cols // LANES, LANES, LANES), F32),
            pltpu.VMEM((cols // LANES, 13, rows, LANES), F32), pltpu.VMEM((12 * rows, cols), F32),
            pltpu.VMEM((24 * SWEEPS, cols), F32), pltpu.VMEM((12 * rows - 24 * SWEEPS, cols), F32),
            pltpu.VMEM((6 * LANES, 2 * LANES), BF16),
        ] + near + near + [
            pltpu.VMEM((12 * rows, 2 * cols), BF16), pltpu.VMEM((2 * LANES, faces), BF16),
            pltpu.VMEM((deep, faces), F32),
            pltpu.VMEM((n, deep, LANES), F32), pltpu.VMEM((n, deep, LANES), F32),
        ] + [pltpu.SemaphoreType.DMA((n,))] * 4 + [pltpu.SemaphoreType.DMA((2, 8))] * 2
        + [pltpu.SemaphoreType.DMA((n,))] * 2
        + [pltpu.VMEM((12, rows, cols), F32), pltpu.SemaphoreType.DMA],
        compiler_params=pltpu.CompilerParams(
            collective_id=1, has_side_effects=True, vmem_limit_bytes=VMEM_LIMIT),
        name="step",
    )(owner, element, state, lift, scale, transfer, stiffness, prev, factor)


def deliver_kernel(disp_ref, face_ref, disp_out, face_out):
    disp_out[...] = disp_ref[...]
    face_out[...] = face_ref[...]


def deliver(disp, face):
    cut = 2
    specs = [pl.BlockSpec((a.shape[0] // cut,) + a.shape[1:], lambda i: (i, 0, 0)) for a in (disp, face)]
    return pl.pallas_call(
        deliver_kernel,
        grid=(cut,),
        in_specs=specs,
        out_specs=specs,
        out_shape=[jax.ShapeDtypeStruct(a.shape, F32) for a in (disp, face)],
        name="deliver",
    )(disp, face)


def local(
    face_owner,
    face_element,
    element_state,
    lift,
    face_scale,
    transfer,
    stiffness_ref,
    element_scale,
    displacement_prev,
):
    n = lax.axis_size("grp") * lax.axis_size("dev")
    faces = face_owner.shape[0]
    cap = -(-(2 * faces // n) // LANES) * LANES
    rows, cols = element_scale.shape
    prev = displacement_prev.reshape(12, rows, cols)
    owner = face_owner.reshape(1, faces)
    disp, face_displacement = outward(
        cap, owner, face_element.reshape(1, faces), element_state, lift,
        face_scale.reshape(1, faces), transfer, stiffness_ref, prev, element_scale,
    )
    disp, face_displacement = deliver(disp, face_displacement)
    return (disp.reshape(4, 3, rows, cols), face_displacement.transpose(1, 0, 2))


def solution(mesh):
    placed = (
        P(("grp", "dev"), None),
        P(("grp", "dev")),
        P(None, ("grp", "dev")),
        P(),
        P(("grp", "dev")),
        P(),
        P(),
        P("grp", "dev"),
        P(None, None, "grp", "dev"),
    )
    return jax.shard_map(
        local,
        mesh=mesh,
        in_specs=placed,
        out_specs=(P(None, None, "grp", "dev"), P(None, None, ("grp", "dev"))),
        check_vma=False,
    )
```

```python
import functools

import jax
import jax.numpy as jnp
from jax import lax
from jax.experimental import pallas as pl
from jax.experimental.pallas import tpu as pltpu
from jax.sharding import PartitionSpec as P

NODES_F = 10
SWEEPS = 8
LANES = 128
VMEM_LIMIT = 56 * 1024 * 1024

coupling_weight = 2.2
highest = lax.Precision.HIGHEST
F32 = jnp.float32
BF16 = jnp.bfloat16
NT = (((1,), (1,)), ((), ()))
VM = pl.BlockSpec(memory_space=pltpu.VMEM)
SM = pl.BlockSpec(memory_space=pltpu.SMEM)


def split(x):
    high = x.astype(BF16).astype(F32)
    return high, x - high


def one_hot(row, count):
    places = lax.broadcasted_iota(jnp.int32, (count, row.shape[1]), 0).astype(F32)
    return jnp.where(places == row, 1.0, 0.0).astype(BF16)


MESH = pl.DeviceIdType.MESH
ANY = pl.BlockSpec(memory_space=pl.ANY)
BLOCK = 8
COLLECT_FAR = False
SPLIT_PART = 0.75
TAKE_FAR = True
CHUNK = 512


def triple(x):
    high = x.astype(BF16)
    rest = x - high.astype(F32)
    middle = rest.astype(BF16)
    return high, middle, (rest - middle.astype(F32)).astype(BF16)


def exact(a, b, dims=(((1,), (0,)), ((), ()))):
    return lax.dot_general(a, b, dims, precision=highest, preferred_element_type=F32)


def same(shape, of_row, of_col):
    left = of_row(lax.broadcasted_iota(jnp.int32, (shape[0], 1), 0))
    return left == of_col(lax.broadcasted_iota(jnp.int32, (1, shape[1]), 1))


def pick(shape, of_row, of_col):
    return jnp.where(same(shape, of_row, of_col), 1.0, 0.0).astype(F32)


def place_of(cap):
    halves = cap // LANES
    return halves, -(-12 * halves // 8) * 8


def identity_of(t, members):
    return (t // members, lax.rem(t, members))


def partner(me, k, n):
    other, bit = 0, 1
    while bit < n:
        a, b = lax.rem(lax.div(me, bit), 2), lax.rem(lax.div(k, bit), 2)
        other = other + bit * (a + b - 2 * a * b)
        bit *= 2
    return other


def turn_of(m, n, members, far_first):
    half, near = n // 2, members // 2
    part, m = lax.div(m, half), lax.rem(m, half)
    top = 1 - part if far_first else part
    row, rows_of = lax.div(m, near) * 2, n // members
    row = lax.rem(row, rows_of) + lax.div(row, rows_of)
    return row * members + top * near + lax.rem(m, near)


def greet_all(n, members, me):
    barrier = pltpu.get_barrier_semaphore()

    def greet(k, carry):
        pl.semaphore_signal(
            barrier, inc=1, device_id=identity_of(lax.rem(me + k, n), members), device_id_type=MESH
        )
        return carry

    lax.fori_loop(1, n, greet, 0)
    return barrier


AROUND = [(1, 0), (-1, 0), (0, 1), (0, -1), (1, 1), (1, -1), (-1, 1), (-1, -1)]
HIGH = 16
SIDE = 8


def node_of(t, q):
    return jnp.where(t == 0, q // 3, 3 - q // 3)


def mixing(inverse, levels):
    def lanes_at(shape, axis):
        lane = lax.broadcasted_iota(jnp.int32, shape, axis)
        t, l = lane // LANES, lane % LANES
        return t, l % 6, jnp.where(l < 6 * levels, l // 6, -1 - axis)

    def ones(condition):
        return jnp.where(condition, 1.0, 0.0).astype(F32)

    wide = 2 * LANES
    t, q, target_level = lanes_at((1, wide), 1)
    to = ones(lax.broadcasted_iota(jnp.int32, (12, wide), 0) == 3 * node_of(t, q) + q % 3)
    t, q, level = lanes_at((wide, 1), 0)
    source = 3 * jnp.where(t == 0, 1 - q // 3, 2 + q // 3) + q % 3
    out = ones(lax.broadcasted_iota(jnp.int32, (wide, 12), 1) == source)
    couple = exact(exact(out, inverse, NT), to) * coupling_weight
    return jnp.where(level == target_level, couple, 0.0)


def stacked(matrix):
    high = matrix.astype(BF16)
    low = (matrix - high.astype(F32)).astype(BF16)
    return jnp.concatenate([high, high, low], axis=0)


def times(x, held):
    high = x.astype(BF16)
    low = (x - high.astype(F32)).astype(BF16)
    return jnp.dot(jnp.concatenate([high, low, high], axis=1), held, preferred_element_type=F32)


def step_kernel(n, groups, members, cap, rows, cols, owner_ref, element_ref, state_ref, lift_ref,
                   scale_ref, transfer_ref, stiff_ref, prev_ref, factor_ref,
                   disp_ref, out_ref,
                   highs, lows, hots, outgoing, incoming, number_out, number_in, rank_ref,
                   shell, other, base, turned, strides, total_load, total_edge, total_inner,
                   couple_held, early, early_in, early_corner, late, late_in, late_corner,
                   table, lane_hots, found, answers, answered,
                   send, recv, number_send, number_recv, near_send, near_recv, back_send, back_recv, disp_held, disp_sem):
    g, d = lax.axis_index("grp"), lax.axis_index("dev")
    me = g * members + d
    faces = owner_ref.shape[1]
    halves, deep = place_of(cap)
    layers = rows // HIGH
    halo = SWEEPS // layers
    levels = HIGH + 2 * halo
    run = 6 * halo
    first_col = 2 * SIDE
    inner = slice(first_col, first_col + cols)

    shell[...] = jnp.zeros_like(shell)
    base[...] = jnp.zeros_like(base)
    turned[...] = jnp.zeros_like(turned)
    barrier = greet_all(n, members, me)

    def component(t, q):
        return 3 * (q // 3 if t == 0 else 3 - q // 3) + q % 3

    lane_tiles = [slice(w * LANES, (w + 1) * LANES) for w in range(cols // LANES)]
    for w, tile in enumerate(lane_tiles):
        strides[w, :12] = prev_ref[:, :, tile]
        strides[w, 12] = 1.0 / factor_ref[:, tile]
    for k in range(layers):
        for t in range(3):
            for w in range(len(lane_tiles)):
                for q in range(6):
                    turned[k * 3 + t, w, pl.ds(run + q, HIGH, stride=6), :] = (
                        strides[w, component(t, q) if t < 2 else 12, pl.ds(k, HIGH, stride=layers), :])
                shell[k, first_col + w * LANES : first_col + (w + 1) * LANES,
                      t * LANES : (t + 1) * LANES] = turned[k * 3 + t, w].T

    stiffness = stiff_ref[...]
    identity = pick((12, 12), lambda i: i, lambda j: j)
    approx = identity / 5.0
    rest = identity - stiffness / 5.0
    for _ in range(8):
        both = exact(jnp.concatenate([approx, rest], axis=0), rest)
        approx, rest = approx + both[:12], both[12:]

    spread = exact(exact(pick((16, 4), lambda i: i // 3, lambda j: j), transfer_ref[...]),
                   pick((NODES_F, 3 * NODES_F), lambda i: i, lambda j: j % NODES_F))
    kept = same(spread.shape, lambda i: i % 3, lambda j: j // NODES_F)
    kept = kept & (lax.broadcasted_iota(jnp.int32, spread.shape, 0) < 12)
    spread = jnp.where(kept, spread, 0.0)[:12]
    spread = jnp.concatenate([exact(approx, spread), jnp.zeros((4, spread.shape[1]), F32)], axis=0)
    gather = jnp.concatenate(triple(exact(spread, lift_ref[...].astype(F32))), axis=0)
    before = jnp.where(
        lax.broadcasted_iota(jnp.int32, (CHUNK, CHUNK), 0)
        < lax.broadcasted_iota(jnp.int32, (CHUNK, CHUNK), 1), 1.0, 0.0
    ).astype(BF16)

    lane = lax.broadcasted_iota(jnp.int32, (1, LANES), 1)

    def lanes_in(start, size):
        return (lane >= start) & (lane < start + size)

    first_half = lax.rem(lane, 6) < 3

    def slot_of(k, t):
        return run * (2 * k + t if t < 2 else 2 * layers + k // 2)

    def pack(ref, tiles, target):
        for v in range(2):
            start = run if v == 1 else 6 * HIGH
            packed = jnp.zeros((cols, LANES), F32)
            for k in range(layers):
                for t in range(tiles):
                    move = slot_of(k, t)
                    turn = (move - start) % LANES
                    piece = ref[k, inner, t * LANES : (t + 1) * LANES]
                    piece = pltpu.roll(piece, turn, 1) if turn else piece
                    wanted = lanes_in(move, run)
                    if t == 2:
                        wanted = wanted & (first_half == (k % 2 == 0))
                    packed = jnp.where(wanted, piece, packed)
            target[v] = packed

    def unpack(ref, tiles, v, arrived, start, size):
        goal = 0 if v == 0 else run + 6 * HIGH
        keep = lanes_in(goal, run)
        for k in range(layers):
            for t in range(tiles):
                turn = (goal - slot_of(k, t)) % LANES
                piece = pltpu.roll(arrived, turn, 1) if turn else arrived
                if t == 2:
                    piece = jnp.where(first_half == (k % 2 == 0), piece,
                                      pltpu.roll(piece, 3 if k % 2 == 0 else LANES - 3, 1))
                here = slice(start, start + size)
                there = slice(t * LANES, (t + 1) * LANES)
                ref[k, here, there] = jnp.where(keep, piece, ref[k, here, there])

    def exists(up, right):
        row, col = g + up, d + right
        return (row >= 0) & (row < groups) & (col >= 0) & (col < members)

    def neighbour_copies(ref, packed, arrived, corner, number):
        copies = []
        for k, (up, right) in enumerate(AROUND):
            v, h = (0 if up == 1 else 1), (0 if right == 1 else 1)
            if right == 0:
                source, target = packed.at[v], arrived.at[v]
            elif up == 0:
                start, end = (cols + SIDE, SIDE) if right == 1 else (first_col, cols + first_col)
                source, target = ref.at[:, pl.ds(start, SIDE), :], ref.at[:, pl.ds(end, SIDE), :]
            else:
                start = cols - SIDE if right == 1 else 0
                source, target = packed.at[v, pl.ds(start, SIDE), :], corner.at[v, h]
            copies.append(pltpu.make_async_remote_copy(
                src_ref=source, dst_ref=target, send_sem=near_send.at[number, k],
                recv_sem=near_recv.at[number, k],
                device_id=(g + up, d + right), device_id_type=MESH))
        return copies

    def begin(copies, kinds):
        for k, (up, right) in enumerate(AROUND):
            if (up == 0) in kinds:
                pl.when(exists(up, right))(copies[k].start)

    def end(copies, ref, tiles, arrived, corner):
        for k, (up, right) in enumerate(AROUND):
            pl.when(exists(up, right))(copies[k].wait_send)
        for v in range(2):

            @pl.when(exists(2 * v - 1, 0))
            def _():
                copies[v].wait_recv()
                unpack(ref, tiles, v, arrived[v], first_col, cols)

        for k, (up, right) in enumerate(AROUND):
            if right != 0:
                pl.when(exists(-up, -right))(copies[k].wait_recv)
        for v in range(2):
            for h in range(2):

                @pl.when(exists(2 * v - 1, 2 * h - 1))
                def _():
                    unpack(ref, tiles, v, corner[v, h], SIDE if h == 0 else cols + first_col, SIDE)

    counts = jnp.zeros((n, 1), F32)
    for i in range(faces // CHUNK):
        here = slice(i * CHUNK, (i + 1) * CHUNK)
        owner_hot = one_hot(owner_ref[:, here].astype(F32), n)
        hot = owner_hot.astype(F32)
        running = jnp.dot(owner_hot, before, preferred_element_type=F32) + counts
        counts = counts + jnp.sum(hot, axis=1, keepdims=True)
        rank = jnp.sum(hot * running, axis=0, keepdims=True)
        rank_ref[:, here] = rank
        hots[:, here] = one_hot(rank, cap)
        parts = jnp.dot(gather, state_ref[:, here], preferred_element_type=F32)
        loads = (parts[:16] + parts[16:32] + parts[32:]) * scale_ref[:, here]
        element = element_ref[:, here]
        high_row = (element // cols).astype(F32)
        low_row = (element % cols).astype(F32)
        where_row = lax.broadcasted_iota(jnp.int32, loads.shape, 0)
        values = jnp.where(where_row == 12, high_row, jnp.where(where_row == 13, low_row, loads))
        high, low = split(values)
        highs[:, here] = high
        lows[:, here] = low
    pack(shell, 3, early)
    pl.semaphore_wait(barrier, n - 1)
    early_copies = neighbour_copies(shell, early, early_in, early_corner, 0)

    def value_copy(owner, slot):
        return pltpu.make_async_remote_copy(
            src_ref=outgoing.at[owner], dst_ref=incoming.at[slot], send_sem=send.at[owner],
            recv_sem=recv.at[slot], device_id=identity_of(owner, members), device_id_type=MESH)

    def number_copy(owner, slot):
        return pltpu.make_async_remote_copy(
            src_ref=number_out.at[owner], dst_ref=number_in.at[slot], send_sem=number_send.at[owner],
            recv_sem=number_recv.at[slot], device_id=identity_of(owner, members), device_id_type=MESH)

    blocks = n // BLOCK

    def send_block(t, carry):
        quarter = max(1, blocks // 4)
        part = lax.div(t, quarter) * 2
        start = ((lax.rem(part, 4) + lax.div(part, 4)) * quarter + lax.rem(t, quarter)) * BLOCK
        owners = [partner(me, turn_of(start + i, n, members, True), n) for i in range(BLOCK)]
        owner_wide = jnp.broadcast_to(owner_ref[...], (16, faces))
        high, low = highs[...], lows[...]
        pieces = []
        for i in range(BLOCK):
            here = owner_wide == owners[i]
            pieces.append(jnp.where(here, high, 0.0).astype(BF16))
            pieces.append(jnp.where(here, low, 0.0).astype(BF16))
        total = lax.dot_general(
            jnp.concatenate(pieces, axis=0), hots[...], NT, preferred_element_type=F32
        )
        for i in range(BLOCK):
            owner = owners[i]
            block = total[32 * i : 32 * i + 16] + total[32 * i + 16 : 32 * i + 32]
            number = (block[12:13] * cols + block[13:14]).astype(jnp.int32)
            lines = [block[:12, h * LANES : (h + 1) * LANES] for h in range(halves)]
            if deep > 12 * halves:
                lines.append(jnp.zeros((deep - 12 * halves, LANES), F32))
            block = jnp.concatenate(lines, axis=0)

            @pl.when(owner == me)
            def _():
                incoming[me] = block
                number_in[me] = number

            @pl.when(owner != me)
            def _():
                outgoing[owner] = block
                number_out[owner] = number
                number_copy(owner, me).start()
                value_copy(owner, me).start()
        return carry

    lax.fori_loop(0, blocks, send_block, 0)
    begin(early_copies, (True, False))
    other[...] = jnp.zeros_like(other)
    couple_held[...] = stacked(mixing(approx, levels))

    def prepare(i, carry):
        here = pl.ds(pl.multiple_of(i * CHUNK, CHUNK), CHUNK)
        rank = rank_ref[:, here].astype(jnp.int32)
        hot = one_hot((rank % LANES).astype(F32), LANES)
        lane_hots[:, here] = jnp.concatenate([hot, hot], axis=0)
        return carry

    lax.fori_loop(0, faces // CHUNK, prepare, 0)

    total_load[...] = jnp.zeros_like(total_load)
    total_edge[...] = jnp.zeros_like(total_edge)
    total_inner[...] = jnp.zeros_like(total_inner)

    per = max(1, min(BLOCK, 1024 // cap))
    width = per * cap

    edge_rows, inner_rows = 12 * 2 * SWEEPS, 12 * (rows - 2 * SWEEPS)

    def level_rows(size, level):
        row = lax.broadcasted_iota(jnp.int32, (size, 1), 0) // 6
        return level(row) * layers

    edge_row = level_rows(2 * run, lambda i: jnp.where(i < halo, i, i + HIGH - 2 * halo))
    inner_row = level_rows(6 * HIGH - 2 * run, lambda i: i + halo)

    def take_sources(t, wait, with_edge, with_inner):
        sources = [partner(me, turn_of(t * per + i, n, members, COLLECT_FAR), n) for i in range(per)]
        if wait:
            for source in sources:

                @pl.when(source != me)
                def _():
                    number_copy(source, source).wait_recv()
                    value_copy(source, source).wait_recv()

        numbers, values = [], []
        for source in sources:
            numbers.append(number_in[source])
            value = incoming[source]
            for h in range(halves):
                values.append(value[12 * h : 12 * h + 12])
        number = jnp.concatenate(numbers, axis=1)
        value = jnp.concatenate(values, axis=1)
        row = number // cols
        low_hot = one_hot((number % cols).astype(F32), cols)
        lefts = []
        for part in split(value):
            tiles = [
                jnp.concatenate([part[component(t, 0) : component(t, 0) + 3],
                                 part[component(t, 3) : component(t, 3) + 3]] * 4, axis=0)
                for t in range(2)
            ]
            pieces = []
            for wanted, level in ((with_edge, edge_row), (with_inner, inner_row)):
                if wanted:
                    for k in range(layers):
                        mask = level + k == row
                        for t in range(2):
                            held = [tiles[t]] * (level.shape[0] // 24)
                            held = jnp.concatenate(held, axis=0) if len(held) > 1 else held[0]
                            pieces.append(jnp.where(mask, held, 0.0))
            lefts.append(jnp.concatenate(pieces, axis=0).astype(BF16))
        left = jnp.concatenate(lefts, axis=1)
        right = jnp.concatenate([low_hot, low_hot], axis=1)
        return lax.dot_general(left, right, NT, preferred_element_type=F32)

    def take_all(t, carry):
        total_load[...] += take_sources(t, True, True, True)
        return carry

    def take_edge(t, carry):
        total_edge[...] += take_sources(t, True, True, False)
        return carry

    def take_inner(t, carry):
        total_inner[...] += take_sources(t, False, False, True)
        return carry

    def placed(value, start, size, target):
        result = None
        for tile in range(start // LANES, (start + size - 1) // LANES + 1):
            end = min((tile + 1) * LANES, value.shape[1])
            piece = value[:, tile * LANES : end]
            if end < (tile + 1) * LANES:
                piece = jnp.concatenate([piece, jnp.zeros((cols, (tile + 1) * LANES - end), F32)], axis=1)
            turn = (target - start) % LANES
            piece = pltpu.roll(piece, turn, 1) if turn else piece
            first, last = max(start, tile * LANES), min(start + size, (tile + 1) * LANES)
            wanted = lanes_in(target + first - start, last - first)
            result = jnp.where(wanted, piece, 0.0 if result is None else result)
        return result

    steps = n // per
    split_at = steps - int(steps * SPLIT_PART)
    lax.fori_loop(0, split_at, take_all, 0)
    lax.fori_loop(split_at, steps, take_edge, 0)
    edge_total = (total_load[:edge_rows] + total_edge[...]).T
    for k in range(layers):
        inv = shell[k, inner, 2 * LANES :]
        for t in range(2):
            start = (2 * k + t) * 2 * run
            value = placed(edge_total, start, run, run) + placed(edge_total, start + run, run, 6 * HIGH)
            base[k, inner, t * LANES : (t + 1) * LANES] = value * inv
    pack(base, 2, late)
    late_copies = neighbour_copies(base, late, late_in, late_corner, 1)
    begin(late_copies, (False,))
    lax.fori_loop(split_at, steps, take_inner, 0)
    inner_total = (total_load[edge_rows:] + total_inner[...]).T
    for k in range(layers):
        inv = shell[k, inner, 2 * LANES :]
        for t in range(2):
            size = 6 * HIGH - 2 * run
            value = placed(inner_total, (2 * k + t) * size, size, 2 * run)
            there = slice(t * LANES, (t + 1) * LANES)
            base[k, inner, there] = base[k, inner, there] + value * inv
    begin(late_copies, (True,))
    end(early_copies, shell, 3, early_in, early_corner)
    end(late_copies, base, 2, late_in, late_corner)

    all_cols = cols + first_col
    here, east, west = (pl.ds(SIDE + move, all_cols) for move in (0, 1, -1))

    def relax(source, target):
        for k in range(layers):
            if k > 0:
                south = source[k - 1, here, LANES : 2 * LANES]
            else:
                south = pltpu.roll(source[layers - 1, here, LANES : 2 * LANES], 6, 1)
            if k < layers - 1:
                north = source[k + 1, here, :LANES]
            else:
                north = pltpu.roll(source[0, here, :LANES], LANES - 6, 1)
            first = jnp.where(first_half, source[k, east, :LANES], source[k, west, :LANES]) + south
            second = jnp.where(
                first_half, source[k, west, LANES : 2 * LANES], source[k, east, LANES : 2 * LANES]
            ) + north
            moved = times(jnp.concatenate([first, second], axis=1), couple_held[...])
            inv = shell[k, here, 2 * LANES :]
            target[k, here, : 2 * LANES] = base[k, here, :] + moved * jnp.concatenate([inv, inv], axis=1)

    def pair(_, carry):
        relax(shell, other)
        relax(other, shell)
        return carry

    lax.fori_loop(0, SWEEPS // 2, pair, 0)

    for k in range(layers):
        for t in range(2):
            for w in range(len(lane_tiles)):
                turned[k * 3 + t, w] = shell[k, first_col + w * LANES : first_col + (w + 1) * LANES,
                                             t * LANES : (t + 1) * LANES].T
                for q in range(6):
                    strides[w, component(t, q), pl.ds(k, HIGH, stride=layers), :] = (
                        turned[k * 3 + t, w, pl.ds(run + q, HIGH, stride=6), :])
    for w, tile in enumerate(lane_tiles):
        value = strides[w, :12]
        disp_held[:, :, tile] = value
        high, low = split(value.reshape(12 * rows, LANES))
        table[:, tile] = high.astype(BF16)
        table[:, cols + w * LANES : cols + (w + 1) * LANES] = low.astype(BF16)
    disp_copy = pltpu.make_async_copy(disp_held, disp_ref, disp_sem)
    disp_copy.start()

    spread = exact(
        pick((8 * NODES_F, NODES_F), lambda i: i // 8, lambda j: j),
        exact(transfer_ref[...], pick((4, 12), lambda i: i, lambda j: j // 3), (((0,), (0,)), ((), ()))),
    )
    spread = jnp.where(same(spread.shape, lambda i: i % 8, lambda j: j % 3), spread, 0.0)

    def back_copy(owner, slot):
        return pltpu.make_async_remote_copy(
            src_ref=answers.at[owner], dst_ref=answered.at[slot], send_sem=back_send.at[owner],
            recv_sem=back_recv.at[slot], device_id=identity_of(owner, members), device_id_type=MESH)

    def answer(t, carry):
        sources = [partner(me, turn_of(t * per + i, n, members, True), n) for i in range(per)]
        number = jnp.concatenate([number_in[source] for source in sources], axis=1)
        mask = lax.broadcasted_iota(jnp.int32, (rows, width), 0) == number // cols
        low_hot = one_hot((number % cols).astype(F32), cols)
        picked = jnp.dot(
            table[...], jnp.concatenate([low_hot, low_hot], axis=0), preferred_element_type=F32
        )
        lines = [
            jnp.sum(jnp.where(mask, picked[c * rows : (c + 1) * rows], 0.0), axis=0, keepdims=True)
            for c in range(12)
        ]
        result = jnp.concatenate(lines, axis=0)
        for i, source in enumerate(sources):
            parts = [
                result[:, i * cap + h * LANES : i * cap + (h + 1) * LANES] for h in range(halves)
            ]
            if deep > 12 * halves:
                parts.append(jnp.zeros((deep - 12 * halves, LANES), F32))
            block = jnp.concatenate(parts, axis=0)

            @pl.when(source == me)
            def _():
                answered[me] = block

            @pl.when(source != me)
            def _():
                answers[source] = block
                back_copy(source, me).start()
        return carry

    lax.fori_loop(0, n // per, answer, 0)

    def take_block(t, carry):
        sources = [partner(me, turn_of(t * BLOCK + i, n, members, TAKE_FAR), n) for i in range(BLOCK)]
        lines = []
        for source in sources:

            @pl.when(source != me)
            def _():
                back_copy(source, source).wait_recv()

            lines.append(answered[source])
        high, low = split(jnp.concatenate(lines, axis=0))
        held = jnp.concatenate([high.astype(BF16), low.astype(BF16)], axis=1)

        for j in range(faces // CHUNK):
            here = slice(j * CHUNK, (j + 1) * CHUNK)
            picked = jnp.dot(held, lane_hots[:, here], preferred_element_type=F32)
            owner = jnp.broadcast_to(owner_ref[:, here], (deep, CHUNK))
            value = found[:, here]
            for i in range(BLOCK):
                value = jnp.where(owner == sources[i], picked[i * deep : (i + 1) * deep], value)
            found[:, here] = value
        return carry

    found[...] = jnp.zeros_like(found)
    lax.fori_loop(0, blocks, take_block, 0)

    high = spread.astype(BF16)
    low = (spread - high.astype(F32)).astype(BF16)
    held = jnp.concatenate([high, high, low], axis=1)
    for j in range(faces // CHUNK):
        here = slice(j * CHUNK, (j + 1) * CHUNK)
        part = rank_ref[:, here].astype(jnp.int32) // LANES
        node = found[:12, here]
        for h in range(1, halves):
            node = jnp.where(part == h, found[12 * h : 12 * h + 12, here], node)
        high = node.astype(BF16)
        low = (node - high.astype(F32)).astype(BF16)
        faced = jnp.dot(
            held, jnp.concatenate([high, low, high], axis=0), preferred_element_type=F32
        )
        for k in range(NODES_F):
            out_ref[k, :, here] = faced[8 * k : 8 * k + 3]

    disp_copy.wait()

    def finish(k, carry):
        owner = lax.rem(me + k, n)
        number_copy(owner, me).wait_send()
        value_copy(owner, me).wait_send()
        back_copy(owner, me).wait_send()
        return carry

    lax.fori_loop(1, n, finish, 0)


def outward(cap, owner, element, state, lift, scale, transfer, stiffness, prev, factor):
    groups, members = lax.axis_size("grp"), lax.axis_size("dev")
    n = groups * members
    faces = owner.shape[1]
    _, rows, cols = prev.shape
    halves, deep = place_of(cap)
    layers = rows // HIGH
    tall = cols + 4 * SIDE
    near = [pltpu.VMEM((2, cols, LANES), F32), pltpu.VMEM((2, cols, LANES), F32),
            pltpu.VMEM((2, 2, SIDE, LANES), F32)]
    return pl.pallas_call(
        functools.partial(step_kernel, n, groups, members, cap, rows, cols),
        in_specs=[VM] * 9,
        out_specs=[ANY, VM],
        out_shape=[jax.ShapeDtypeStruct((12, rows, cols), F32),
                   jax.ShapeDtypeStruct((NODES_F, 3, faces), F32)],
        scratch_shapes=[
            pltpu.VMEM((16, faces), F32), pltpu.VMEM((16, faces), F32), pltpu.VMEM((cap, faces), BF16),
            pltpu.VMEM((n, deep, LANES), F32), pltpu.VMEM((n, deep, LANES), F32),
            pltpu.VMEM((n, 1, cap), jnp.int32), pltpu.VMEM((n, 1, cap), jnp.int32),
            pltpu.VMEM((1, faces), F32),
            pltpu.VMEM((layers, tall, 3 * LANES), F32), pltpu.VMEM((layers, tall, 2 * LANES), F32),
            pltpu.VMEM((layers, tall, 2 * LANES), F32), pltpu.VMEM((3 * layers, cols // LANES, LANES, LANES), F32),
            pltpu.VMEM((cols // LANES, 13, rows, LANES), F32), pltpu.VMEM((12 * rows, cols), F32),
            pltpu.VMEM((24 * SWEEPS, cols), F32), pltpu.VMEM((12 * rows - 24 * SWEEPS, cols), F32),
            pltpu.VMEM((6 * LANES, 2 * LANES), BF16),
        ] + near + near + [
            pltpu.VMEM((12 * rows, 2 * cols), BF16), pltpu.VMEM((2 * LANES, faces), BF16),
            pltpu.VMEM((deep, faces), F32),
            pltpu.VMEM((n, deep, LANES), F32), pltpu.VMEM((n, deep, LANES), F32),
        ] + [pltpu.SemaphoreType.DMA((n,))] * 4 + [pltpu.SemaphoreType.DMA((2, 8))] * 2
        + [pltpu.SemaphoreType.DMA((n,))] * 2
        + [pltpu.VMEM((12, rows, cols), F32), pltpu.SemaphoreType.DMA],
        compiler_params=pltpu.CompilerParams(
            collective_id=1, has_side_effects=True, vmem_limit_bytes=VMEM_LIMIT),
        name="step",
    )(owner, element, state, lift, scale, transfer, stiffness, prev, factor)


def deliver_kernel(disp_ref, face_ref, disp_out, face_out):
    disp_out[...] = disp_ref[...]
    face_out[...] = face_ref[...]


def deliver(disp, face):
    cut = 2
    specs = [pl.BlockSpec((a.shape[0] // cut,) + a.shape[1:], lambda i: (i, 0, 0)) for a in (disp, face)]
    return pl.pallas_call(
        deliver_kernel,
        grid=(cut,),
        in_specs=specs,
        out_specs=specs,
        out_shape=[jax.ShapeDtypeStruct(a.shape, F32) for a in (disp, face)],
        name="deliver",
    )(disp, face)


def local(
    face_owner,
    face_element,
    element_state,
    lift,
    face_scale,
    transfer,
    stiffness_ref,
    element_scale,
    displacement_prev,
):
    n = lax.axis_size("grp") * lax.axis_size("dev")
    faces = face_owner.shape[0]
    cap = -(-(2 * faces // n) // LANES) * LANES
    rows, cols = element_scale.shape
    prev = displacement_prev.reshape(12, rows, cols)
    owner = face_owner.reshape(1, faces)
    disp, face_displacement = outward(
        cap, owner, face_element.reshape(1, faces), element_state, lift,
        face_scale.reshape(1, faces), transfer, stiffness_ref, prev, element_scale,
    )
    disp, face_displacement = deliver(disp, face_displacement)
    return (disp.reshape(4, 3, rows, cols), face_displacement.transpose(1, 0, 2))


def solution(mesh):
    placed = (
        P(("grp", "dev"), None),
        P(("grp", "dev")),
        P(None, ("grp", "dev")),
        P(),
        P(("grp", "dev")),
        P(),
        P(),
        P("grp", "dev"),
        P(None, None, "grp", "dev"),
    )
    return jax.shard_map(
        local,
        mesh=mesh,
        in_specs=placed,
        out_specs=(P(None, None, "grp", "dev"), P(None, None, ("grp", "dev"))),
        check_vma=False,
    )
```
